256 devices in a mesh: leaf: 4 (over y), frow: 16 (over z, x_lo), fcol: 4 (over x_hi, core).
Axes of the slice: x: 4 (x_hi: 2, x_lo: 2; x = x_hi * 2 + x_lo), y: 4, z: 8, core: 2. Of those that a mesh axis runs over, the one named last changes fastest.
Arguments:
- child_fronts: float32 [4, 4096, 4096], P('leaf', 'frow', 'fcol'), may hold values from -20 to 120, as said below
- parent_front: float32 [4096, 4096], P('frow', 'fcol'), may hold values from -20 to 120, as said below
- block_maps: int32 [4, 32], P('leaf'), may hold values from 0 to 31, as said below
Outputs:
- child_factors: float32 [4, 4096, 4096], P('leaf', 'frow', 'fcol')
- parent_factor: float32 [4096, 4096], P('frow', 'fcol')
The draws below stay inside these ranges and needn't reach their ends.
Inputs may be any that keep to these rules, and one draw needn't show every extreme that they name: Each row block_maps[l] is a permutation of the block numbers that keeps every block inside its group of 2 consecutive blocks: block_maps[l, i] // 2 == i // 2. `child_fronts`: every child front is symmetric positive definite. `parent_front`: the parent front is symmetric positive definite.
All inputs are finite; a program needn't handle non-finite values.
Results may differ from the reference program's by a relative error of at most 0.0001.
Values sent between devices are 32-bit elements; how exact they have to be, the bound alone decides.
No kernel may reach another device: no remote copies, remote signals or barrier semaphores. Data moves between devices by JAX's collectives and lax.ppermute only.
A program may use at most 64 MiB of HBM per device.

```python
import math
import jax
import jax.numpy as jnp
from jax import lax

BLOCK = 128
FRONT = 4096
CHILD_PANELS = 2
PARENT_PANELS = 1
CHILDREN = 4
BLOCKS = 32
GROUP = 2


common_rank = 256


common_weight = 2.0


def symmetric_base(key, members, lowest, highest):
    noise_key = jax.random.fold_in(key, 31)
    diagonal_key = jax.random.fold_in(key, 37)
    common_key = jax.random.fold_in(key, 43)
    half_width = 0.5 * math.sqrt(3.0 / FRONT)
    uniform_noise = jax.random.uniform(noise_key, (members, FRONT, FRONT), jnp.float32, -half_width, half_width)
    symmetric = (uniform_noise + jnp.swapaxes(uniform_noise, 1, 2)) * 0.5
    factors = jax.random.uniform(common_key, (members, FRONT, common_rank), jnp.float32, -math.sqrt(3.0), math.sqrt(3.0))
    shared = jnp.einsum('mik,mjk->mij', factors, factors, precision=lax.Precision.HIGHEST) * (common_weight / common_rank)
    shared = (shared + jnp.swapaxes(shared, 1, 2)) * 0.5
    diagonal = jax.random.uniform(diagonal_key, (members, FRONT), jnp.float32, lowest, highest)
    identity = jnp.eye(FRONT, dtype=jnp.float32)
    return symmetric + shared + diagonal[:, :, None] * identity[None, :, :]


def draw_child_fronts(key, part):
    matrix = symmetric_base(jax.random.fold_in(key, 11), CHILDREN, 2.0, 4.0)
    return matrix


def draw_parent_front(key, part):
    matrix = symmetric_base(jax.random.fold_in(key, 21), 1, 1.0, 2.0)
    return matrix[0]


def draw_block_maps(key, part):
    scores = jax.random.randint(jax.random.fold_in(key, 41), (CHILDREN, BLOCKS), 0, 4096)
    slot_index = jnp.arange(BLOCKS, dtype=jnp.int32)
    grouped = slot_index // GROUP * (4096 * BLOCKS) + scores * BLOCKS + slot_index[None, :]
    return jnp.argsort(grouped, axis=1).astype(jnp.int32)


def setup_inputs(seed: int = 0) -> dict:
    keys = jax.random.split(jax.random.key(seed), 4)
    return {
        "child_fronts": draw_child_fronts(jax.random.fold_in(keys[3], 71), 0),
        "parent_front": draw_parent_front(jax.random.fold_in(keys[3], 71), 0),
        "block_maps": draw_block_maps(jax.random.fold_in(keys[3], 71), 0),
    }


def partial_factor(matrix, panels):
    for number in range(panels):
        first_col = number * BLOCK
        end_col = first_col + BLOCK
        factor = jnp.linalg.cholesky(matrix[first_col:end_col, first_col:end_col])
        lower_rows = lax.linalg.triangular_solve(factor, matrix[end_col:, first_col:end_col], left_side=False, lower=True, transpose_a=True)
        column = jnp.concatenate([jnp.zeros((first_col, BLOCK), jnp.float32), factor, lower_rows], axis=0)
        matrix = matrix.at[:, first_col:end_col].set(column)
        matrix = matrix.at[first_col:end_col, end_col:].set(0.0)
        matrix = matrix.at[end_col:, end_col:].add(-jnp.dot(lower_rows, lower_rows.T, precision=lax.Precision.HIGHEST))
    return matrix

def reference(child_fronts, parent_front, block_maps):
    positions = jnp.arange(FRONT, dtype=jnp.int32)
    trailing = positions >= CHILD_PANELS * BLOCK
    assembled = parent_front
    factored = []
    for child_index in range(CHILDREN):
        finished = partial_factor(child_fronts[child_index], CHILD_PANELS)
        factored.append(finished)
        target = (block_maps[child_index][positions // BLOCK] * BLOCK + positions % BLOCK).astype(jnp.int32)
        contribution = jnp.where(trailing[:, None] & trailing[None, :], finished, 0.0)
        assembled = assembled.at[target[:, None], target[None, :]].add(contribution)
    return (jnp.stack(factored), partial_factor(assembled, PARENT_PANELS))
```

```python
import jax
import jax.numpy as jnp
from jax import lax
from jax.sharding import PartitionSpec as P

BLOCK = 128
PIVOTS = 256
HIGHEST = lax.Precision.HIGHEST
PLANE = ("frow", "fcol")
ROWS = 16
COLS = 4


def mm(a, b):
    return lax.dot_general(a, b, (((1,), (0,)), ((), ())), precision=HIGHEST)


def mm_t(a, b):
    return lax.dot_general(a, b, (((1,), (1,)), ((), ())), precision=HIGHEST)


def at(r, c):
    return r * COLS + c


def spread_rows(x, r):
    for step in (8, 4, 2, 1):
        sources = [q for q in range(0, ROWS, 2 * step)]
        pairs = [(at(q, 0), at(q + step, 0)) for q in sources]
        got = lax.ppermute(x, PLANE, pairs)
        target = (r % (2 * step)) == step
        x = jnp.where(target, got, x)
    return x


def spread_cols(x, c):
    got = lax.ppermute(x, PLANE, [(at(q, 0), at(q, 2)) for q in range(ROWS)])
    x = jnp.where(c == 2, got, x)
    got = lax.ppermute(x, PLANE, [(at(q, k), at(q, k + 1)) for q in range(ROWS) for k in (0, 2)])
    return jnp.where(c % 2 == 1, got, x)


def gathered_panel(panel, parent_panel, leaf):
    pieces = []
    r_of = lambda k, i: k * 4 + i
    piece = jnp.zeros((72, PIVOTS), jnp.float32)
    for j in range(4):
        own = panel[64 * j : 64 * j + 64]
        mine = lax.dynamic_slice_in_dim(parent_panel, 64 * leaf + 16 * j, 16).reshape(8, PIVOTS)
        sent = jnp.concatenate([own, mine], axis=0)
        pairs = [(at(4 * k + i, 0), at(4 * i + j, k)) for k in range(COLS) for i in range(4)]
        piece = piece + lax.ppermute(sent, PLANE, pairs)
    copies = jnp.broadcast_to(piece[None], (ROWS, 72, PIVOTS))
    everything = lax.all_to_all(copies, "frow", 0, 0, tiled=True)
    child = everything[:, :64].reshape(1024, PIVOTS)
    parent = everything[:, 64:].reshape(4, 4, 16, BLOCK)
    return child, parent


def swapped(x, flags, dim):
    groups = flags.shape[0]
    shape = x.shape
    view = x.reshape(*shape[:dim], groups, 2, BLOCK, *shape[dim + 1 :])
    other = jnp.flip(view, axis=dim + 1)
    pick = flags.reshape((1,) * dim + (groups,) + (1,) * (view.ndim - dim - 1))
    return jnp.where(pick, other, view).reshape(shape)


def sum_over_leaf(block, leaf):
    def exchange(x, pairs):
        return lax.ppermute(x, "leaf", pairs)

    near = [(0, 1), (1, 0), (2, 3), (3, 2)]
    far = [(0, 3), (3, 0), (1, 2), (2, 1)]
    mid = jnp.where((leaf == 1) | (leaf == 2), 1, 0)
    high = leaf // 2
    low = leaf % 2
    half = block.shape[0] // 2
    lines = (
        (block[:half], near, far, mid, high),
        (block[half:], far, near, high, low),
    )
    cut = half // 2
    first = []
    for x, one, two, f, s in lines:
        first.append(exchange(lax.dynamic_slice_in_dim(x, (1 - f) * cut, cut), one))
    sums = []
    for (x, one, two, f, s), got in zip(lines, first):
        sums.append(lax.dynamic_slice_in_dim(x, f * cut, cut) + got)
    small = cut // 2
    second = []
    for (x, one, two, f, s), acc in zip(lines, sums):
        second.append(exchange(lax.dynamic_slice_in_dim(acc, (1 - s) * small, small), two))
    done = []
    for (x, one, two, f, s), acc, got in zip(lines, sums, second):
        done.append(lax.dynamic_slice_in_dim(acc, s * small, small) + got)
    third = [exchange(d, line[2]) for d, line in zip(done, lines)]
    halves = []
    for (x, one, two, f, s), d, got in zip(lines, done, third):
        halves.append(jnp.where(s == 0, jnp.concatenate([d, got]), jnp.concatenate([got, d])))
    fourth = [exchange(h, line[1]) for h, line in zip(halves, lines)]
    whole = []
    for (x, one, two, f, s), h, got in zip(lines, halves, fourth):
        whole.append(jnp.where(f == 0, jnp.concatenate([h, got]), jnp.concatenate([got, h])))
    return jnp.concatenate(whole)


def factor_128(a):
    k = lax.linalg.cholesky(a, symmetrize_input=False)
    inv = lax.linalg.triangular_solve(k, jnp.eye(BLOCK, dtype=jnp.float32), left_side=True, lower=True)
    return jnp.tril(k), inv


def per_device(child_fronts, parent_front, block_maps):
    leaf = lax.axis_index("leaf")
    r = lax.axis_index("frow")
    c = lax.axis_index("fcol")
    front = child_fronts[0]
    maps = block_maps[0]

    panel = front[:, :PIVOTS]
    parent_panel = parent_front[:, :BLOCK]

    first = spread_rows(panel[:BLOCK, :BLOCK], r)
    rest = spread_rows(jnp.concatenate([panel[BLOCK:], parent_panel[:BLOCK]], axis=1), r)
    first = spread_cols(first, c)
    rest = spread_cols(rest, c)
    rows = spread_cols(jnp.concatenate([panel, parent_panel], axis=1), c)
    own_rows = rows[:, :PIVOTS]
    own_parent_rows = rows[:, PIVOTS:]
    col_rows, parent_cols = gathered_panel(panel, parent_panel, leaf)

    kp, kp_inv = factor_128(rest[:, PIVOTS:])
    k1, k1_inv = factor_128(first)
    k21 = mm_t(rest[:, :BLOCK], k1_inv)
    k2, k2_inv = factor_128(rest[:, BLOCK:PIVOTS] - mm_t(k21, k21))
    zero = jnp.zeros((BLOCK, BLOCK), jnp.float32)
    k21_inv = -mm(k2_inv, mm(k21, k1_inv))
    k_inv = jnp.concatenate(
        [jnp.concatenate([k1_inv, zero], axis=1), jnp.concatenate([k21_inv, k2_inv], axis=1)], axis=0
    )
    k = jnp.concatenate([jnp.concatenate([k1, zero], axis=1), jnp.concatenate([k21, k2], axis=1)], axis=0)

    b_rows = mm_t(own_rows, k_inv)
    b_cols = mm_t(col_rows, k_inv)

    bp_rows = mm_t(own_parent_rows, kp_inv)
    row_number = 256 * r + jnp.arange(256, dtype=jnp.int32)[:, None]
    col_number = 1024 * c + jnp.arange(1024, dtype=jnp.int32)[None, :]
    strip = (col_number // 64) % 4 == leaf
    mine = jnp.arange(4, dtype=jnp.int32) == leaf
    spread_strip = jnp.where(
        mine[None, :, None, None, None], parent_cols[:, None], 0.0
    ).reshape(1024, BLOCK)
    bp_cols = mm_t(spread_strip, kp_inv)
    parent_top = jnp.concatenate([kp, bp_rows[BLOCK:]], axis=0)
    parent_left = jnp.where(r == 0, parent_top, bp_rows)
    parent_part = parent_front - mm_t(bp_rows, bp_cols)
    parent_part = jnp.where(row_number >= BLOCK, parent_part, 0.0)
    left = jnp.where(c == 0, parent_left, parent_part[:, :BLOCK])
    parent_part = jnp.concatenate([left, parent_part[:, BLOCK:]], axis=1)
    parent_part = jnp.where(strip, parent_part, 0.0)

    targets = maps.reshape(16, 2)
    flags = targets[:, 0] % 2 == 1
    row_flag = lax.dynamic_slice_in_dim(flags, r, 1)
    col_flags = lax.dynamic_slice_in_dim(flags, 4 * c, 4)
    kept = (row_number >= PIVOTS) & (col_number >= PIVOTS)
    moved = swapped(swapped(front, row_flag, 0), col_flags, 1)
    moved_rows = swapped(b_rows, row_flag, 0)
    moved_cols = swapped(b_cols, col_flags, 0)
    contribution = jnp.where(kept, moved - mm_t(moved_rows, moved_cols), 0.0)
    parent_done = sum_over_leaf(contribution + parent_part, leaf)

    finished = jnp.where(row_number >= PIVOTS, front - mm_t(b_rows, b_cols), 0.0)
    child_left = jnp.where(r == 0, k, b_rows)
    child_left = jnp.where(c == 0, child_left, finished[:, :PIVOTS])
    finished = jnp.concatenate([child_left, finished[:, PIVOTS:]], axis=1)
    return (finished[None], parent_done)


def solution(mesh):
    return jax.shard_map(
        per_device,
        mesh=mesh,
        in_specs=(P("leaf", "frow", "fcol"), P("frow", "fcol"), P("leaf", None)),
        out_specs=(P("leaf", "frow", "fcol"), P("frow", "fcol")),
        check_vma=False,
    )
```

```python
import functools

import jax
import jax.numpy as jnp
from jax import lax
from jax.experimental import pallas as pl
from jax.experimental.pallas import tpu as pltpu
from jax.sharding import PartitionSpec as P

BLOCK = 128
PIVOTS = 256
PLANE = ("frow", "fcol")
ROWS = 16
COLS = 4
HIGHEST = lax.Precision.HIGHEST
VMEM = pl.BlockSpec(memory_space=pltpu.VMEM)
SMEM = pl.BlockSpec(memory_space=pltpu.SMEM)


def mm(a, b):
    return lax.dot_general(
        a, b, (((1,), (0,)), ((), ())), precision=HIGHEST, preferred_element_type=jnp.float32
    )


def mm_t(a, b):
    return lax.dot_general(
        a, b, (((1,), (1,)), ((), ())), precision=HIGHEST, preferred_element_type=jnp.float32
    )


def f32(*shape):
    return jax.ShapeDtypeStruct(shape, jnp.float32)


def eight_columns(groups, start):
    lane = lax.broadcasted_iota(jnp.int32, (8, BLOCK), 1)
    sub = lax.broadcasted_iota(jnp.int32, (8, BLOCK), 0)
    spread = lambda v: jnp.broadcast_to(v, (8, BLOCK))
    here = start // 8
    inside = (lane >= start) & (lane < start + 8)
    x = groups[here]
    column = [spread(x[:, start + k : start + k + 1]) for k in range(8)]
    s = [[spread(column[k][i : i + 1]) if k <= i else None for k in range(8)] for i in range(8)]
    unit = jnp.where(inside, jnp.where(lane - start == sub, 1.0, 0.0), x)
    line = [spread(unit[k : k + 1]) for k in range(8)]
    inv = [None] * 8
    low = [[None] * 8 for _ in range(8)]
    forward = [None] * 8
    for k in range(8):
        inv[k] = 1.0 / s[k][k]
        for i in range(k + 1, 8):
            low[i][k] = s[i][k] * inv[k]
        for i in range(k + 1, 8):
            for q in range(k + 1, i + 1):
                s[i][q] = s[i][q] - low[i][k] * s[q][k]
        t = line[k]
        for q in range(k):
            t = t - low[k][q] * forward[q]
        forward[k] = t
    back = [None] * 8
    for k in reversed(range(8)):
        t = inv[k] * forward[k]
        for i in range(k + 1, 8):
            t = t - low[i][k] * back[i]
        back[k] = t
    for g in range(here + 1, BLOCK // 8):
        rows = groups[g]
        parts = [spread(rows[:, start + k : start + k + 1]) * back[k] for k in range(8)]
        while len(parts) > 1:
            parts = [parts[i] + parts[i + 1] for i in range(0, len(parts), 2)]
        groups[g] = jnp.where(inside, 0.0, rows) - parts[0]
    own = forward[0] * jnp.sqrt(inv[0])
    for k in range(1, 8):
        own = jnp.where(sub == k, forward[k] * jnp.sqrt(inv[k]), own)
    groups[here] = own


def inverse_factors(blocks):
    split = [[b[8 * g : 8 * g + 8] for g in range(BLOCK // 8)] for b in blocks]
    for start in range(0, BLOCK, 8):
        for groups in split:
            eight_columns(groups, start)
    row, col = square()
    return [jnp.where(col <= row, jnp.concatenate(groups, axis=0), 0.0) for groups in split]


def square():
    shape = (BLOCK, BLOCK)
    return lax.broadcasted_iota(jnp.int32, shape, 0), lax.broadcasted_iota(jnp.int32, shape, 1)


def pack_body(front, parent, pivots, rows, *scattered):
    leaf = lax.axis_index("leaf")
    row, col = square()
    a11 = front[0, :BLOCK, :BLOCK]
    a22 = front[0, BLOCK:, BLOCK:]
    pivots[:BLOCK] = jnp.where(col <= row, a11, a22)
    pivots[BLOCK:PIVOTS] = front[0, BLOCK:, :BLOCK]
    pivots[PIVOTS : PIVOTS + BLOCK] = parent[:BLOCK]
    diag = jnp.sum(jnp.where(row == col, a22, 0.0), axis=0, keepdims=True)
    pivots[PIVOTS + BLOCK :] = jnp.broadcast_to(diag, (8, BLOCK))
    rows[:, :PIVOTS] = front[0]
    rows[:, PIVOTS:] = parent[...]
    for j, out in enumerate(scattered):
        out[:64] = front[0, 64 * j : 64 * j + 64]
        at_row = pl.multiple_of(64 * leaf + 16 * j, 8)
        out[64:, :BLOCK] = parent[pl.ds(at_row, 8)]
        out[64:, BLOCK:] = parent[pl.ds(at_row + 8, 8)]


def pack(front, parent):
    return pl.pallas_call(
        pack_body,
        grid=(1,),
        in_specs=[
            pl.BlockSpec((1, PIVOTS, PIVOTS), lambda i: (0, 0, 0)),
            pl.BlockSpec((PIVOTS, BLOCK), lambda i: (0, 0)),
        ],
        out_specs=[VMEM] * 6,
        out_shape=[f32(392, BLOCK), f32(256, 384)] + [f32(72, PIVOTS)] * 4,
        name="pack",
    )(front, parent)


def factor_body(pivots, k, k_inv, kp, kp_inv):
    row, col = square()
    both = pivots[:BLOCK]
    low = jnp.where(col <= row, both, 0.0)
    a11 = low + jnp.where(col < row, low, 0.0).T
    high = jnp.where(col > row, both, 0.0)
    diag = jnp.broadcast_to(pivots[PIVOTS + BLOCK : PIVOTS + BLOCK + 1], (BLOCK, BLOCK))
    a22 = high + high.T + jnp.where(row == col, diag, 0.0)
    a21 = pivots[BLOCK:PIVOTS]
    ap = pivots[PIVOTS : PIVOTS + BLOCK]
    (k1_inv,) = inverse_factors([a11])
    k21 = mm_t(a21, k1_inv)
    s22 = a22 - mm_t(k21, k21)
    k2_inv, parent_inv = inverse_factors([s22, ap])
    zero = jnp.zeros((BLOCK, BLOCK), jnp.float32)
    k_inv[:BLOCK, :BLOCK] = k1_inv
    k_inv[:BLOCK, BLOCK:] = zero
    k_inv[BLOCK:, :BLOCK] = -mm(k2_inv, mm(k21, k1_inv))
    k_inv[BLOCK:, BLOCK:] = k2_inv
    k[:BLOCK, :BLOCK] = jnp.where(col <= row, mm_t(a11, k1_inv), 0.0)
    k[:BLOCK, BLOCK:] = zero
    k[BLOCK:, :BLOCK] = k21
    k[BLOCK:, BLOCK:] = jnp.where(col <= row, mm_t(s22, k2_inv), 0.0)
    kp_inv[...] = parent_inv
    kp[...] = jnp.where(col <= row, mm_t(ap, parent_inv), 0.0)


def factor(pivots):
    return pl.pallas_call(
        factor_body,
        in_specs=[VMEM],
        out_specs=[VMEM] * 4,
        out_shape=[f32(PIVOTS, PIVOTS)] * 2 + [f32(BLOCK, BLOCK)] * 2,
        name="factor",
    )(pivots)


def contribute_body(
    maps, rows, gathered, k_inv, kp, kp_inv, front, parent, out, b_rows, b_cols, lines, columns
):
    leaf, r, c = lax.axis_index("leaf"), lax.axis_index("frow"), lax.axis_index("fcol")
    kept_rows = jnp.where(r > 0, 1.0, 0.0)
    b = mm_t(rows[:, :PIVOTS], k_inv[...])
    b_rows[...] = b
    turn = maps[0, 2 * r] % 2
    for h in range(2):
        lines[pl.ds(pl.multiple_of((h + turn) % 2 * BLOCK, BLOCK), BLOCK), :PIVOTS] = (
            b[h * BLOCK : (h + 1) * BLOCK] * kept_rows
        )
    bp = mm_t(rows[:, PIVOTS:], kp_inv[...])
    lines[:BLOCK, PIVOTS:] = bp[:BLOCK] * kept_rows
    lines[BLOCK:, PIVOTS:] = bp[BLOCK:]
    columns[:, PIVOTS:] = jnp.zeros((1024, BLOCK), jnp.float32)
    pair = lax.broadcasted_iota(jnp.int32, (1, BLOCK), 1)

    @pl.loop(0, 4)
    def _(i):
        at = pl.multiple_of(256 * i, 256)
        kept = jnp.where((c > 0) | (i > 0), 1.0, 0.0)
        group = 4 * c + i
        swap = maps[0, 2 * group] % 2
        raw = jnp.concatenate([gathered[4 * i + j, :64] for j in range(4)], axis=0)
        own = mm_t(raw, k_inv[...])
        b_cols[pl.ds(at, 256)] = own
        for h in range(2):
            to = pl.multiple_of(at + (h + swap) % 2 * BLOCK, BLOCK)
            columns[pl.ds(to, BLOCK), :PIVOTS] = own[h * BLOCK : (h + 1) * BLOCK] * kept
        strip = jnp.concatenate(
            [gathered[4 * i + j, 64:, half : half + BLOCK] for j in range(4) for half in (0, BLOCK)],
            axis=0,
        )
        pivot_strip = (c == 0) & (i == 0) & (leaf < 2)
        to = pl.multiple_of(at + 64 * leaf, 64)
        columns[pl.ds(to, 64), PIVOTS:] = mm_t(strip, kp_inv[...]) * jnp.where(pivot_strip, 0.0, 1.0)
        update = mm_t(lines[...], columns[pl.ds(at, 256)])
        for h in range(2):
            from_row = pl.multiple_of((h + turn) % 2 * BLOCK, BLOCK)
            for g in range(2):
                from_col = pl.multiple_of(at + (g + swap) % 2 * BLOCK, BLOCK)
                to_col = pl.multiple_of(at + g * BLOCK, BLOCK)
                mine = (2 * g + pair // 64) == leaf
                child = front[0, pl.ds(from_row, BLOCK), pl.ds(from_col, BLOCK)] * (kept_rows * kept)
                theirs = parent[h * BLOCK : (h + 1) * BLOCK, pl.ds(to_col, BLOCK)]
                if h == 0:
                    theirs = theirs * kept_rows
                value = child + jnp.where(mine, theirs, 0.0)
                out[h * BLOCK : (h + 1) * BLOCK, pl.ds(to_col, BLOCK)] = (
                    value - update[h * BLOCK : (h + 1) * BLOCK, g * BLOCK : (g + 1) * BLOCK]
                )

    @pl.when(c == 0)
    def _():
        mine = pair // 64 == leaf
        top = jnp.where(r == 0, kp[...], bp[:BLOCK])
        out[:BLOCK, :BLOCK] = jnp.where(mine, top, 0.0)
        out[BLOCK:, :BLOCK] = jnp.where(mine, bp[BLOCK:], 0.0)


def contribute(maps, rows, gathered, k_inv, kp, kp_inv, front, parent):
    return pl.pallas_call(
        contribute_body,
        in_specs=[SMEM] + [VMEM] * 7,
        out_specs=[VMEM] * 3,
        out_shape=[f32(256, 1024), f32(256, 256), f32(1024, 256)],
        scratch_shapes=[pltpu.VMEM((256, 384), jnp.float32), pltpu.VMEM((1024, 384), jnp.float32)],
        name="contribute",
    )(maps, rows, gathered, k_inv, kp, kp_inv, front, parent)


def finish_body(front, b_rows, b_cols, k, out):
    r, c = lax.axis_index("frow"), lax.axis_index("fcol")

    @pl.when(r == 0)
    def _():
        out[...] = jnp.zeros_like(out)

    @pl.when(r > 0)
    def _():
        @pl.loop(0, 4)
        def _(i):
            at = pl.multiple_of(256 * i, 256)
            out[0, :, pl.ds(at, 256)] = front[0, :, pl.ds(at, 256)] - mm_t(
                b_rows[...], b_cols[pl.ds(at, 256)]
            )

    @pl.when(c == 0)
    def _():
        out[0, :, :PIVOTS] = jnp.where(r == 0, k[...], b_rows[...])


def finish(front, b_rows, b_cols, k):
    return pl.pallas_call(
        finish_body,
        in_specs=[VMEM] * 4,
        out_specs=VMEM,
        out_shape=f32(1, 256, 1024),
        cost_estimate=pl.CostEstimate(flops=6 * 2 * 256 * 256 * 1024, bytes_accessed=4 << 20, transcendentals=0),
        name="finish",
    )(front, b_rows, b_cols, k)


def at(r, c):
    return r * COLS + c


def spread_pivots(x, r, c):
    for step in (8, 4, 2, 1):
        pairs = [(at(q, 0), at(q + step, 0)) for q in range(0, ROWS, 2 * step)]
        got = lax.ppermute(x, PLANE, pairs)
        x = jnp.where(r % (2 * step) == step, got, x)
    return spread_cols(x, c)


def spread_cols(x, c):
    got = lax.ppermute(x, PLANE, [(at(q, 0), at(q, 2)) for q in range(ROWS)])
    x = jnp.where(c == 2, got, x)
    got = lax.ppermute(x, PLANE, [(at(q, k), at(q, k + 1)) for q in range(ROWS) for k in (0, 2)])
    return jnp.where(c % 2 == 1, got, x)


def gather_columns(scattered):
    piece = None
    for j, sent in enumerate(scattered):
        pairs = [(at(4 * k + i, 0), at(4 * i + j, k)) for k in range(COLS) for i in range(4)]
        got = lax.ppermute(sent, PLANE, pairs)
        piece = got if piece is None else piece + got
    copies = jnp.broadcast_to(piece[None], (ROWS, 72, PIVOTS))
    return lax.all_to_all(copies, "frow", 0, 0, tiled=True)


def sum_over_leaf(block, leaf):
    def exchange(x, pairs):
        return lax.ppermute(x, "leaf", pairs)

    near = [(0, 1), (1, 0), (2, 3), (3, 2)]
    far = [(0, 3), (3, 0), (1, 2), (2, 1)]
    mid = jnp.where((leaf == 1) | (leaf == 2), 1, 0)
    high = leaf // 2
    low = leaf % 2
    half = block.shape[0] // 2
    lines = (
        (block[:half], near, far, mid, high),
        (block[half:], far, near, high, low),
    )
    cut = half // 2
    first = []
    for x, one, two, f, s in lines:
        first.append(exchange(lax.dynamic_slice_in_dim(x, (1 - f) * cut, cut), one))
    sums = []
    for (x, one, two, f, s), got in zip(lines, first):
        sums.append(lax.dynamic_slice_in_dim(x, f * cut, cut) + got)
    small = cut // 2
    second = []
    for (x, one, two, f, s), acc in zip(lines, sums):
        second.append(exchange(lax.dynamic_slice_in_dim(acc, (1 - s) * small, small), two))
    done = []
    for (x, one, two, f, s), acc, got in zip(lines, sums, second):
        done.append(lax.dynamic_slice_in_dim(acc, s * small, small) + got)
    third = [exchange(d, line[2]) for d, line in zip(done, lines)]
    halves = []
    for (x, one, two, f, s), d, got in zip(lines, done, third):
        halves.append(jnp.where(s == 0, jnp.concatenate([d, got]), jnp.concatenate([got, d])))
    fourth = [exchange(h, line[1]) for h, line in zip(halves, lines)]
    whole = []
    for (x, one, two, f, s), h, got in zip(lines, halves, fourth):
        whole.append(jnp.where(f == 0, jnp.concatenate([h, got]), jnp.concatenate([got, h])))
    return jnp.concatenate(whole)


def per_device(child_fronts, parent_front, block_maps):
    leaf = lax.axis_index("leaf")
    r = lax.axis_index("frow")
    c = lax.axis_index("fcol")
    pivots, rows, *scattered = pack(child_fronts, parent_front)
    with jax.named_scope("pivots"):
        pivots = spread_pivots(pivots, r, c)
    with jax.named_scope("columns"):
        gathered = gather_columns(scattered)
    with jax.named_scope("rows"):
        rows = spread_cols(rows, c)
    k, k_inv, kp, kp_inv = factor(pivots)
    part, b_rows, b_cols = contribute(
        block_maps, rows, gathered, k_inv, kp, kp_inv, child_fronts, parent_front
    )
    with jax.named_scope("leafsum"):
        parent_done = sum_over_leaf(part, leaf)
    return finish(child_fronts, b_rows, b_cols, k), parent_done


def solution(mesh):
    return jax.shard_map(
        per_device,
        mesh=mesh,
        in_specs=(P("leaf", "frow", "fcol"), P("frow", "fcol"), P("leaf", None)),
        out_specs=(P("leaf", "frow", "fcol"), P("frow", "fcol")),
        check_vma=False,
    )
```

```python
import jax
import jax.numpy as jnp
from jax import lax
from jax.experimental import pallas as pl
from jax.experimental.pallas import tpu as pltpu
from jax.sharding import PartitionSpec as P


BLOCK = 128
PIVOTS = 256
PLANE = ("frow", "fcol")
ROWS = 16
COLS = 4
HIGHEST = lax.Precision.HIGHEST
VMEM = pl.BlockSpec(memory_space=pltpu.VMEM)
SMEM = pl.BlockSpec(memory_space=pltpu.SMEM)


def mm(a, b):
    return lax.dot_general(
        a, b, (((1,), (0,)), ((), ())), precision=HIGHEST, preferred_element_type=jnp.float32
    )


def mm_t(a, b):
    return lax.dot_general(
        a, b, (((1,), (1,)), ((), ())), precision=HIGHEST, preferred_element_type=jnp.float32
    )


def halves(x):
    high = x.astype(jnp.bfloat16)
    return high, (x - high.astype(jnp.float32)).astype(jnp.bfloat16)


def product_t(a, b):
    dot = lambda x, y: lax.dot_general(
        x, y, (((1,), (1,)), ((), ())), preferred_element_type=jnp.float32
    )
    (ah, al), (bh, bl) = a, b
    return dot(ah, bh) + (dot(ah, bl) + dot(al, bh))


def f32(*shape):
    return jax.ShapeDtypeStruct(shape, jnp.float32)


def eight_columns(groups, start):
    lane = lax.broadcasted_iota(jnp.int32, (8, BLOCK), 1)
    sub = lax.broadcasted_iota(jnp.int32, (8, BLOCK), 0)
    spread = lambda v: jnp.broadcast_to(v, (8, BLOCK))
    here = start // 8
    inside = (lane >= start) & (lane < start + 8)
    x = groups[here]
    column = [spread(x[:, start + k : start + k + 1]) for k in range(8)]
    s = [[spread(column[k][i : i + 1]) if k <= i else None for k in range(8)] for i in range(8)]
    unit = jnp.where(inside, jnp.where(lane - start == sub, 1.0, 0.0), x)
    line = [spread(unit[k : k + 1]) for k in range(8)]
    inv = [None] * 8
    low = [[None] * 8 for _ in range(8)]
    forward = [None] * 8
    for k in range(8):
        inv[k] = 1.0 / s[k][k]
        for i in range(k + 1, 8):
            low[i][k] = s[i][k] * inv[k]
        for i in range(k + 1, 8):
            for q in range(k + 1, i + 1):
                s[i][q] = s[i][q] - low[i][k] * s[q][k]
        t = line[k]
        for q in range(k):
            t = t - low[k][q] * forward[q]
        forward[k] = t
    back = [None] * 8
    for k in reversed(range(8)):
        t = inv[k] * forward[k]
        for i in range(k + 1, 8):
            t = t - low[i][k] * back[i]
        back[k] = t
    for g in range(here + 1, BLOCK // 8):
        rows = groups[g]
        parts = [spread(rows[:, start + k : start + k + 1]) * back[k] for k in range(8)]
        while len(parts) > 1:
            parts = [parts[i] + parts[i + 1] for i in range(0, len(parts), 2)]
        groups[g] = jnp.where(inside, 0.0, rows) - parts[0]
    own = forward[0] * jnp.sqrt(inv[0])
    for k in range(1, 8):
        own = jnp.where(sub == k, forward[k] * jnp.sqrt(inv[k]), own)
    groups[here] = own


def inverse_factors(blocks):
    split = [[b[8 * g : 8 * g + 8] for g in range(BLOCK // 8)] for b in blocks]
    for start in range(0, BLOCK, 8):
        for groups in split:
            eight_columns(groups, start)
    row, col = square()
    return [jnp.where(col <= row, jnp.concatenate(groups, axis=0), 0.0) for groups in split]


def square():
    shape = (BLOCK, BLOCK)
    return lax.broadcasted_iota(jnp.int32, shape, 0), lax.broadcasted_iota(jnp.int32, shape, 1)


def pack_body(front, parent, pivots, rows, *scattered):
    leaf = lax.axis_index("leaf")
    row, col = square()
    a11 = front[0, :BLOCK, :BLOCK]
    a22 = front[0, BLOCK:, BLOCK:]
    pivots[:BLOCK] = jnp.where(col <= row, a11, a22)
    pivots[BLOCK:PIVOTS] = front[0, BLOCK:, :BLOCK]
    pivots[PIVOTS : PIVOTS + BLOCK] = parent[:BLOCK]
    diag = jnp.sum(jnp.where(row == col, a22, 0.0), axis=0, keepdims=True)
    pivots[PIVOTS + BLOCK :] = jnp.broadcast_to(diag, (8, BLOCK))
    rows[:, :PIVOTS] = front[0]
    rows[:, PIVOTS:] = parent[...]
    for j, out in enumerate(scattered):
        out[:64] = front[0, 64 * j : 64 * j + 64]
        at_row = pl.multiple_of(64 * leaf + 16 * j, 8)
        out[64:, :BLOCK] = parent[pl.ds(at_row, 8)]
        out[64:, BLOCK:] = parent[pl.ds(at_row + 8, 8)]


def pack(front, parent):
    return pl.pallas_call(
        pack_body,
        grid=(1,),
        in_specs=[
            pl.BlockSpec((1, PIVOTS, PIVOTS), lambda i: (0, 0, 0)),
            pl.BlockSpec((PIVOTS, BLOCK), lambda i: (0, 0)),
        ],
        out_specs=[VMEM] * 6,
        out_shape=[f32(392, BLOCK), f32(256, 384)] + [f32(72, PIVOTS)] * 4,
        name="pack",
    )(front, parent)


def factor_body(pivots, k, k_inv, kp, kp_inv):
    row, col = square()
    both = pivots[:BLOCK]
    low = jnp.where(col <= row, both, 0.0)
    a11 = low + jnp.where(col < row, low, 0.0).T
    high = jnp.where(col > row, both, 0.0)
    diag = jnp.broadcast_to(pivots[PIVOTS + BLOCK : PIVOTS + BLOCK + 1], (BLOCK, BLOCK))
    a22 = high + high.T + jnp.where(row == col, diag, 0.0)
    a21 = pivots[BLOCK:PIVOTS]
    ap = pivots[PIVOTS : PIVOTS + BLOCK]
    (k1_inv,) = inverse_factors([a11])
    k21 = mm_t(a21, k1_inv)
    s22 = a22 - mm_t(k21, k21)
    k2_inv, parent_inv = inverse_factors([s22, ap])
    zero = jnp.zeros((BLOCK, BLOCK), jnp.float32)
    k_inv[:BLOCK, :BLOCK] = k1_inv
    k_inv[:BLOCK, BLOCK:] = zero
    k_inv[BLOCK:, :BLOCK] = -mm(k2_inv, mm(k21, k1_inv))
    k_inv[BLOCK:, BLOCK:] = k2_inv
    k[:BLOCK, :BLOCK] = jnp.where(col <= row, mm_t(a11, k1_inv), 0.0)
    k[:BLOCK, BLOCK:] = zero
    k[BLOCK:, :BLOCK] = k21
    k[BLOCK:, BLOCK:] = jnp.where(col <= row, mm_t(s22, k2_inv), 0.0)
    kp_inv[...] = parent_inv
    kp[...] = jnp.where(col <= row, mm_t(ap, parent_inv), 0.0)


def factor(pivots):
    return pl.pallas_call(
        factor_body,
        in_specs=[VMEM],
        out_specs=[VMEM] * 4,
        out_shape=[f32(PIVOTS, PIVOTS)] * 2 + [f32(BLOCK, BLOCK)] * 2,
        name="factor",
    )(pivots)


def raw_columns(gathered):
    return jnp.concatenate([gathered[j, :64] for j in range(4)], axis=0)


def contribute_body(
    maps, rows, gathered, k_inv, kp, kp_inv, front, parent, *rest
):
    outs, (lines_high, lines_low, columns, value) = rest[:4], rest[4:]
    leaf, r, c = lax.axis_index("leaf"), lax.axis_index("frow"), lax.axis_index("fcol")
    i = pl.program_id(0)
    kept_rows = jnp.where(r > 0, 1.0, 0.0)
    turn = maps[0, 2 * r] % 2

    @pl.when(i == 0)
    def _():
        b = mm_t(rows[:, :PIVOTS], k_inv[...]) * kept_rows
        bp = mm_t(rows[:, PIVOTS:], kp_inv[...])
        for h in range(2):
            block = slice(h * BLOCK, (h + 1) * BLOCK)
            to = pl.multiple_of((h + turn) % 2 * BLOCK, BLOCK)
            lines_high[pl.ds(to, BLOCK), :PIVOTS], lines_low[pl.ds(to, BLOCK), :PIVOTS] = halves(b[block])
            mine = bp[block] * kept_rows if h == 0 else bp[block]
            lines_high[block, PIVOTS:], lines_low[block, PIVOTS:] = halves(mine)
        columns[:, PIVOTS:] = jnp.zeros((256, BLOCK), jnp.float32)

    pair = lax.broadcasted_iota(jnp.int32, (1, BLOCK), 1)
    kept = jnp.where((c > 0) | (i > 0), 1.0, 0.0)
    swap = maps[0, 2 * (4 * c + i)] % 2
    own = mm_t(raw_columns(gathered), k_inv[...])
    for h in range(2):
        to = pl.multiple_of((h + swap) % 2 * BLOCK, BLOCK)
        columns[pl.ds(to, BLOCK), :PIVOTS] = own[h * BLOCK : (h + 1) * BLOCK] * kept
    strip = jnp.concatenate(
        [gathered[j, 64:, half : half + BLOCK] for j in range(4) for half in (0, BLOCK)], axis=0
    )
    pivot_strip = (c == 0) & (i == 0) & (leaf < 2)
    to = pl.multiple_of(64 * leaf, 64)
    columns[pl.ds(to, 64), PIVOTS:] = mm_t(strip, kp_inv[...]) * jnp.where(pivot_strip, 0.0, 1.0)
    update = product_t((lines_high[...], lines_low[...]), halves(columns[...]))
    for h in range(2):
        from_row = pl.multiple_of((h + turn) % 2 * BLOCK, BLOCK)
        block = slice(h * BLOCK, (h + 1) * BLOCK)
        for g in range(2):
            from_col = pl.multiple_of((g + swap) % 2 * BLOCK, BLOCK)
            strips = slice(g * BLOCK, (g + 1) * BLOCK)
            mine = (2 * g + pair // 64) == leaf
            child = front[0, pl.ds(from_row, BLOCK), pl.ds(from_col, BLOCK)] * (kept_rows * kept)
            theirs = parent[block, strips]
            if h == 0:
                theirs = theirs * kept_rows
            value[block, strips] = child + jnp.where(mine, theirs, 0.0) - update[block, strips]

    @pl.when((c == 0) & (i == 0))
    def _():
        mine = pair // 64 == leaf
        bp = mm_t(rows[:, PIVOTS:], kp_inv[...])
        top = jnp.where(r == 0, kp[...], bp[:BLOCK])
        value[:BLOCK, :BLOCK] = jnp.where(mine, top, 0.0)
        value[BLOCK:, :BLOCK] = jnp.where(mine, bp[BLOCK:], 0.0)

    for half, bit in enumerate(first_bits(leaf)):
        for out, at_row in ((outs[2 * half], 1 - bit), (outs[2 * half + 1], bit)):
            out[...] = value[pl.ds(pl.multiple_of(BLOCK * half + 64 * at_row, 64), 64)]


def first_bits(leaf):
    return jnp.where((leaf == 1) | (leaf == 2), 1, 0), leaf // 2


def whole(*shape):
    return pl.BlockSpec(shape, lambda i: (0,) * len(shape))


GATHERED = pl.BlockSpec((4, 72, PIVOTS), lambda i: (i, 0, 0))
FRONT = pl.BlockSpec((1, 256, 256), lambda i: (0, 0, i))
PARENT = pl.BlockSpec((256, 256), lambda i: (0, i))


def contribute(maps, rows, gathered, k_inv, kp, kp_inv, front, parent):
    return pl.pallas_call(
        contribute_body,
        grid=(4,),
        in_specs=[
            SMEM,
            whole(256, 384),
            GATHERED,
            whole(PIVOTS, PIVOTS),
            whole(BLOCK, BLOCK),
            whole(BLOCK, BLOCK),
            FRONT,
            PARENT,
        ],
        out_specs=[pl.BlockSpec((64, 256), lambda i: (0, i))] * 4,
        out_shape=[f32(64, 1024)] * 4,
        scratch_shapes=[
            pltpu.VMEM((256, 384), jnp.bfloat16),
            pltpu.VMEM((256, 384), jnp.bfloat16),
            pltpu.VMEM((256, 384), jnp.float32),
            pltpu.VMEM((256, 256), jnp.float32),
        ],
        name="contribute",
    )(maps, rows, gathered, k_inv, kp, kp_inv, front, parent)


def finish_body(rows, gathered, k, k_inv, front, out, b_rows, high, low):
    r, c = lax.axis_index("frow"), lax.axis_index("fcol")
    i = pl.program_id(0)

    @pl.when(i == 0)
    def _():
        b = mm_t(rows[:, :PIVOTS], k_inv[...])
        b_rows[...] = b
        high[...], low[...] = halves(b)

    @pl.when(r == 0)
    def _():
        out[...] = jnp.zeros_like(out)

    @pl.when(r > 0)
    def _():
        own = mm_t(raw_columns(gathered), k_inv[...])
        out[0] = front[0] - product_t((high[...], low[...]), halves(own))

    @pl.when((c == 0) & (i == 0))
    def _():
        out[0] = jnp.where(r == 0, k[...], b_rows[...])


def finish(rows, gathered, k, k_inv, front):
    return pl.pallas_call(
        finish_body,
        grid=(4,),
        in_specs=[
            whole(256, 384),
            GATHERED,
            whole(PIVOTS, PIVOTS),
            whole(PIVOTS, PIVOTS),
            FRONT,
        ],
        out_specs=FRONT,
        out_shape=f32(1, 256, 1024),
        scratch_shapes=[
            pltpu.VMEM((256, 256), jnp.float32),
            pltpu.VMEM((256, 256), jnp.bfloat16),
            pltpu.VMEM((256, 256), jnp.bfloat16),
        ],
        cost_estimate=pl.CostEstimate(flops=1 << 31, bytes_accessed=4 << 20, transcendentals=0),
        name="finish",
    )(rows, gathered, k, k_inv, front)


def at(r, c):
    return r * COLS + c


def spread_rows(x, r, steps):
    for step in steps:
        pairs = [(at(q, 0), at(q + step, 0)) for q in range(0, ROWS, 2 * step)]
        got = lax.ppermute(x, PLANE, pairs)
        x = jnp.where(r % (2 * step) == step, got, x)
    return x


def spread_far(x, c):
    got = lax.ppermute(x, PLANE, [(at(q, 0), at(q, 2)) for q in range(ROWS)])
    return jnp.where(c == 2, got, x)


def spread_core(x, c):
    got = lax.ppermute(x, PLANE, [(at(q, k), at(q, k + 1)) for q in range(ROWS) for k in (0, 2)])
    return jnp.where(c % 2 == 1, got, x)


def scatter_columns(scattered):
    piece = None
    for j, sent in enumerate(scattered):
        pairs = [(at(4 * k + i, 0), at(4 * i + j, k)) for k in range(COLS) for i in range(4)]
        got = lax.ppermute(sent, PLANE, pairs)
        piece = got if piece is None else piece + got
    return piece


def gather_columns(piece):
    copies = jnp.broadcast_to(piece[None], (ROWS, 72, PIVOTS))
    return lax.all_to_all(copies, "frow", 0, 0, tiled=True)


def sum_over_leaf(parts, leaf):
    near = [(0, 1), (1, 0), (2, 3), (3, 2)]
    far = [(0, 3), (3, 0), (1, 2), (2, 1)]
    upper, lower = first_bits(leaf)
    sends, keeps = parts[0::2], parts[1::2]
    pairs = ((near, far), (far, near))
    first = (upper, lower)
    second = (leaf // 2, leaf % 2)

    def exchange(xs, turn):
        return [lax.ppermute(x, "leaf", p[turn]) for x, p in zip(xs, pairs)]

    def ordered(bit, mine, got):
        return jnp.where(bit == 0, jnp.concatenate([mine, got]), jnp.concatenate([got, mine]))

    got = exchange(sends, 0)
    sums = [x + y for x, y in zip(keeps, got)]
    small = 32
    cut = lambda x, i: lax.dynamic_slice_in_dim(x, i * small, small)
    got = exchange([cut(x, 1 - b) for x, b in zip(sums, second)], 1)
    done = [cut(x, b) + y for x, b, y in zip(sums, second, got)]
    got = exchange(done, 1)
    halved = [ordered(b, x, y) for b, x, y in zip(second, done, got)]
    got = exchange(halved, 0)
    return jnp.concatenate([ordered(b, x, y) for b, x, y in zip(first, halved, got)])


def per_device(child_fronts, parent_front, block_maps):
    leaf = lax.axis_index("leaf")
    r = lax.axis_index("frow")
    c = lax.axis_index("fcol")
    pivots, rows, *scattered = pack(child_fronts, parent_front)
    pivots = spread_rows(pivots, r, (8, 4, 2))
    rows = spread_far(rows, c)
    piece = scatter_columns(scattered)
    gathered = gather_columns(piece)
    pivots = spread_rows(pivots, r, (1,))
    pivots = spread_far(pivots, c)
    pivots = spread_core(pivots, c)
    rows = spread_core(rows, c)
    k, k_inv, kp, kp_inv = factor(pivots)
    parts = contribute(
        block_maps, rows, gathered, k_inv, kp, kp_inv, child_fronts, parent_front
    )
    parent_done = sum_over_leaf(parts, leaf)
    return finish(rows, gathered, k, k_inv, child_fronts), parent_done


def solution(mesh):
    return jax.shard_map(
        per_device,
        mesh=mesh,
        in_specs=(P("leaf", "frow", "fcol"), P("frow", "fcol"), P("leaf", None)),
        out_specs=(P("leaf", "frow", "fcol"), P("frow", "fcol")),
        check_vma=False,
    )
```

```python
import jax
import jax.numpy as jnp
from jax import lax
from jax.experimental import pallas as pl
from jax.experimental.pallas import tpu as pltpu
from jax.sharding import PartitionSpec as P


BLOCK = 128
PIVOTS = 256
PLANE = ("frow", "fcol")
ROWS = 16
COLS = 4
HIGHEST = lax.Precision.HIGHEST
VMEM = pl.BlockSpec(memory_space=pltpu.VMEM)
SMEM = pl.BlockSpec(memory_space=pltpu.SMEM)


def mm(a, b):
    return lax.dot_general(
        a, b, (((1,), (0,)), ((), ())), precision=HIGHEST, preferred_element_type=jnp.float32
    )


def mm_t(a, b):
    return lax.dot_general(
        a, b, (((1,), (1,)), ((), ())), precision=HIGHEST, preferred_element_type=jnp.float32
    )


def halves(x):
    high = x.astype(jnp.bfloat16)
    return high, (x - high.astype(jnp.float32)).astype(jnp.bfloat16)


def product_t(a, b):
    dot = lambda x, y: lax.dot_general(
        x, y, (((1,), (1,)), ((), ())), preferred_element_type=jnp.float32
    )
    (ah, al), (bh, bl) = a, b
    return dot(ah, bh) + (dot(ah, bl) + dot(al, bh))


def f32(*shape):
    return jax.ShapeDtypeStruct(shape, jnp.float32)


def eight_columns(groups, start):
    lane = lax.broadcasted_iota(jnp.int32, (8, BLOCK), 1)
    sub = lax.broadcasted_iota(jnp.int32, (8, BLOCK), 0)
    spread = lambda v: jnp.broadcast_to(v, (8, BLOCK))
    here = start // 8
    inside = (lane >= start) & (lane < start + 8)
    x = groups[here]
    column = [spread(x[:, start + k : start + k + 1]) for k in range(8)]
    s = [[spread(column[k][i : i + 1]) if k <= i else None for k in range(8)] for i in range(8)]
    unit = jnp.where(inside, jnp.where(lane - start == sub, 1.0, 0.0), x)
    line = [spread(unit[k : k + 1]) for k in range(8)]
    inv = [None] * 8
    low = [[None] * 8 for _ in range(8)]
    forward = [None] * 8
    for k in range(8):
        inv[k] = 1.0 / s[k][k]
        for i in range(k + 1, 8):
            low[i][k] = s[i][k] * inv[k]
        for i in range(k + 1, 8):
            for q in range(k + 1, i + 1):
                s[i][q] = s[i][q] - low[i][k] * s[q][k]
        t = line[k]
        for q in range(k):
            t = t - low[k][q] * forward[q]
        forward[k] = t
    back = [None] * 8
    for k in reversed(range(8)):
        t = inv[k] * forward[k]
        for i in range(k + 1, 8):
            t = t - low[i][k] * back[i]
        back[k] = t
    for g in range(here + 1, BLOCK // 8):
        rows = groups[g]
        parts = [spread(rows[:, start + k : start + k + 1]) * back[k] for k in range(8)]
        while len(parts) > 1:
            parts = [parts[i] + parts[i + 1] for i in range(0, len(parts), 2)]
        groups[g] = jnp.where(inside, 0.0, rows) - parts[0]
    own = forward[0] * jnp.sqrt(inv[0])
    for k in range(1, 8):
        own = jnp.where(sub == k, forward[k] * jnp.sqrt(inv[k]), own)
    groups[here] = own


def inverse_factors(blocks):
    split = [[b[8 * g : 8 * g + 8] for g in range(BLOCK // 8)] for b in blocks]
    for start in range(0, BLOCK, 8):
        for groups in split:
            eight_columns(groups, start)
    row, col = square()
    return [jnp.where(col <= row, jnp.concatenate(groups, axis=0), 0.0) for groups in split]


def square():
    shape = (BLOCK, BLOCK)
    return lax.broadcasted_iota(jnp.int32, shape, 0), lax.broadcasted_iota(jnp.int32, shape, 1)


def pack_body(front, parent, pivots, k, kp, rows, *scattered):
    leaf, r, c = lax.axis_index("leaf"), lax.axis_index("frow"), lax.axis_index("fcol")
    rows[:, :PIVOTS] = front[0]
    rows[:, PIVOTS:] = parent[...]
    for j, out in enumerate(scattered):
        out[:64] = front[0, 64 * j : 64 * j + 64]
        at_row = pl.multiple_of(64 * leaf + 16 * j, 8)
        out[64:, :BLOCK] = parent[pl.ds(at_row, 8)]
        out[64:, BLOCK:] = parent[pl.ds(at_row + 8, 8)]
    owner = (r == 0) & (c == 0)

    @pl.when(owner)
    def _():
        row, col = square()
        a11 = front[0, :BLOCK, :BLOCK]
        ap = parent[:BLOCK]
        (k1_inv,) = inverse_factors([a11])
        k21 = mm_t(front[0, BLOCK:, :BLOCK], k1_inv)
        s22 = front[0, BLOCK:, BLOCK:] - mm_t(k21, k21)
        k2_inv, parent_inv = inverse_factors([s22, ap])
        pivots[:BLOCK] = jnp.where(col <= row, k1_inv, k2_inv.T)
        pivots[BLOCK:PIVOTS] = -mm(k2_inv, mm(k21, k1_inv))
        pivots[PIVOTS : PIVOTS + BLOCK] = parent_inv
        diag = jnp.sum(jnp.where(row == col, k2_inv, 0.0), axis=0, keepdims=True)
        pivots[PIVOTS + BLOCK :] = jnp.broadcast_to(diag, (8, BLOCK))
        k[:BLOCK, :BLOCK] = jnp.where(col <= row, mm_t(a11, k1_inv), 0.0)
        k[:BLOCK, BLOCK:] = jnp.zeros((BLOCK, BLOCK), jnp.float32)
        k[BLOCK:, :BLOCK] = k21
        k[BLOCK:, BLOCK:] = jnp.where(col <= row, mm_t(s22, k2_inv), 0.0)
        kp[...] = jnp.where(col <= row, mm_t(ap, parent_inv), 0.0)

    @pl.when(jnp.logical_not(owner))
    def _():
        for out in (pivots, k, kp):
            out[...] = jnp.zeros_like(out)


def pack(front, parent):
    return pl.pallas_call(
        pack_body,
        grid=(1,),
        in_specs=[
            pl.BlockSpec((1, PIVOTS, PIVOTS), lambda i: (0, 0, 0)),
            pl.BlockSpec((PIVOTS, BLOCK), lambda i: (0, 0)),
        ],
        out_specs=[VMEM] * 8,
        out_shape=[f32(392, BLOCK), f32(PIVOTS, PIVOTS), f32(BLOCK, BLOCK), f32(256, 384)]
        + [f32(72, PIVOTS)] * 4,
        name="pack",
    )(front, parent)


def prepare_body(
    maps, pivots, kp, rows, front, parent, base, high, low, b_rows, k_inv, kp_inv
):
    leaf, r, c = lax.axis_index("leaf"), lax.axis_index("frow"), lax.axis_index("fcol")
    i = pl.program_id(0)
    kept_rows = jnp.where(r > 0, 1.0, 0.0)
    turn = maps[0, 2 * r] % 2

    @pl.when(i == 0)
    def _():
        row, col = square()
        both = pivots[:BLOCK]
        diag = jnp.broadcast_to(pivots[PIVOTS + BLOCK : PIVOTS + BLOCK + 1], (BLOCK, BLOCK))
        k_inv[:BLOCK, :BLOCK] = jnp.where(col <= row, both, 0.0)
        k_inv[:BLOCK, BLOCK:] = jnp.zeros((BLOCK, BLOCK), jnp.float32)
        k_inv[BLOCK:, :BLOCK] = pivots[BLOCK:PIVOTS]
        k_inv[BLOCK:, BLOCK:] = jnp.where(col > row, both, 0.0).T + jnp.where(row == col, diag, 0.0)
        kp_inv[...] = pivots[PIVOTS : PIVOTS + BLOCK]
        b = mm_t(rows[:, :PIVOTS], k_inv[...])
        b_rows[:, :PIVOTS] = b
        b = b * kept_rows
        bp = mm_t(rows[:, PIVOTS:], kp_inv[...])
        b_rows[:, PIVOTS:] = bp
        for h in range(2):
            block = slice(h * BLOCK, (h + 1) * BLOCK)
            to = pl.multiple_of((h + turn) % 2 * BLOCK, BLOCK)
            high[pl.ds(to, BLOCK), :PIVOTS], low[pl.ds(to, BLOCK), :PIVOTS] = halves(b[block])
            mine = bp[block] * kept_rows if h == 0 else bp[block]
            high[block, PIVOTS:], low[block, PIVOTS:] = halves(mine)

    pair = lax.broadcasted_iota(jnp.int32, (1, BLOCK), 1)
    kept = jnp.where((c > 0) | (i > 0), 1.0, 0.0)
    swap = maps[0, 2 * (4 * c + i)] % 2
    for h in range(2):
        from_row = pl.multiple_of((h + turn) % 2 * BLOCK, BLOCK)
        block = slice(h * BLOCK, (h + 1) * BLOCK)
        for g in range(2):
            from_col = pl.multiple_of((g + swap) % 2 * BLOCK, BLOCK)
            strips = slice(g * BLOCK, (g + 1) * BLOCK)
            mine = (2 * g + pair // 64) == leaf
            child = front[0, pl.ds(from_row, BLOCK), pl.ds(from_col, BLOCK)] * (kept_rows * kept)
            theirs = parent[block, strips]
            if h == 0:
                theirs = theirs * kept_rows
            base[block, strips] = child + jnp.where(mine, theirs, 0.0)

    @pl.when((c == 0) & (i == 0))
    def _():
        mine = pair // 64 == leaf
        top = jnp.where(r == 0, kp[...], b_rows[:BLOCK, PIVOTS:])
        base[:BLOCK, :BLOCK] = jnp.where(mine, top, 0.0)
        base[BLOCK:, :BLOCK] = jnp.where(mine, b_rows[BLOCK:, PIVOTS:], 0.0)


def whole(*shape):
    return pl.BlockSpec(shape, lambda i: (0,) * len(shape))


GATHERED = pl.BlockSpec((4, 72, PIVOTS), lambda i: (i, 0, 0))
FRONT = pl.BlockSpec((1, 256, 256), lambda i: (0, 0, i))
PARENT = pl.BlockSpec((256, 256), lambda i: (0, i))


def prepare(maps, pivots, kp, rows, front, parent):
    half = jax.ShapeDtypeStruct((256, 384), jnp.bfloat16)
    return pl.pallas_call(
        prepare_body,
        grid=(4,),
        in_specs=[SMEM, whole(392, BLOCK), whole(BLOCK, BLOCK), whole(256, 384), FRONT, PARENT],
        out_specs=[
            PARENT,
            whole(256, 384),
            whole(256, 384),
            whole(256, 384),
            whole(PIVOTS, PIVOTS),
            whole(BLOCK, BLOCK),
        ],
        out_shape=[f32(256, 1024), half, half, f32(256, 384), f32(PIVOTS, PIVOTS), f32(BLOCK, BLOCK)],
        name="prepare",
    )(maps, pivots, kp, rows, front, parent)


def raw_columns(gathered):
    return jnp.concatenate([gathered[j, :64] for j in range(4)], axis=0)


def contribute_body(maps, gathered, k_inv, kp_inv, base, high, low, *rest):
    outs, (columns, value) = rest[:4], rest[4:]
    leaf, c = lax.axis_index("leaf"), lax.axis_index("fcol")
    i = pl.program_id(0)

    @pl.when(i == 0)
    def _():
        columns[:, PIVOTS:] = jnp.zeros((256, BLOCK), jnp.float32)

    kept = jnp.where((c > 0) | (i > 0), 1.0, 0.0)
    swap = maps[0, 2 * (4 * c + i)] % 2
    own = mm_t(raw_columns(gathered), k_inv[...])
    for h in range(2):
        to = pl.multiple_of((h + swap) % 2 * BLOCK, BLOCK)
        columns[pl.ds(to, BLOCK), :PIVOTS] = own[h * BLOCK : (h + 1) * BLOCK] * kept
    strip = jnp.concatenate(
        [gathered[j, 64:, half : half + BLOCK] for j in range(4) for half in (0, BLOCK)], axis=0
    )
    pivot_strip = (c == 0) & (i == 0) & (leaf < 2)
    to = pl.multiple_of(64 * leaf, 64)
    columns[pl.ds(to, 64), PIVOTS:] = mm_t(strip, kp_inv[...]) * jnp.where(pivot_strip, 0.0, 1.0)
    value[...] = base[...] - product_t((high[...], low[...]), halves(columns[...]))
    for half, bit in enumerate(first_bits(leaf)):
        for out, at_row in ((outs[2 * half], 1 - bit), (outs[2 * half + 1], bit)):
            out[...] = value[pl.ds(pl.multiple_of(BLOCK * half + 64 * at_row, 64), 64)]


def first_bits(leaf):
    return jnp.where((leaf == 1) | (leaf == 2), 1, 0), leaf // 2


def contribute(maps, gathered, k_inv, kp_inv, base, high, low):
    return pl.pallas_call(
        contribute_body,
        grid=(4,),
        in_specs=[
            SMEM,
            GATHERED,
            whole(PIVOTS, PIVOTS),
            whole(BLOCK, BLOCK),
            PARENT,
            whole(256, 384),
            whole(256, 384),
        ],
        out_specs=[pl.BlockSpec((64, 256), lambda i: (0, i))] * 4,
        out_shape=[f32(64, 1024)] * 4,
        scratch_shapes=[pltpu.VMEM((256, 384), jnp.float32), pltpu.VMEM((256, 256), jnp.float32)],
        name="contribute",
    )(maps, gathered, k_inv, kp_inv, base, high, low)


def finish_body(b_rows, gathered, k, k_inv, front, out, high, low):
    r, c = lax.axis_index("frow"), lax.axis_index("fcol")
    i = pl.program_id(0)

    @pl.when(i == 0)
    def _():
        high[...], low[...] = halves(b_rows[:, :PIVOTS])

    @pl.when(r == 0)
    def _():
        out[...] = jnp.zeros_like(out)

    @pl.when(r > 0)
    def _():
        own = mm_t(raw_columns(gathered), k_inv[...])
        out[0] = front[0] - product_t((high[...], low[...]), halves(own))

    @pl.when((c == 0) & (i == 0))
    def _():
        out[0] = jnp.where(r == 0, k[...], b_rows[:, :PIVOTS])


def finish(b_rows, gathered, k, k_inv, front):
    return pl.pallas_call(
        finish_body,
        grid=(4,),
        in_specs=[
            whole(256, 384),
            GATHERED,
            whole(PIVOTS, PIVOTS),
            whole(PIVOTS, PIVOTS),
            FRONT,
        ],
        out_specs=FRONT,
        out_shape=f32(1, 256, 1024),
        scratch_shapes=[
            pltpu.VMEM((256, 256), jnp.bfloat16),
            pltpu.VMEM((256, 256), jnp.bfloat16),
        ],
        cost_estimate=pl.CostEstimate(flops=1 << 31, bytes_accessed=4 << 20, transcendentals=0),
        name="finish",
    )(b_rows, gathered, k, k_inv, front)


def at(r, c):
    return r * COLS + c


def spread_rows(x, r, steps):
    for step in steps:
        pairs = [(at(q, 0), at(q + step, 0)) for q in range(0, ROWS, 2 * step)]
        got = lax.ppermute(x, PLANE, pairs)
        x = jnp.where(r % (2 * step) == step, got, x)
    return x


def spread_far(x, c):
    got = lax.ppermute(x, PLANE, [(at(q, 0), at(q, 2)) for q in range(ROWS)])
    return jnp.where(c == 2, got, x)


def spread_core(x, c):
    got = lax.ppermute(x, PLANE, [(at(q, k), at(q, k + 1)) for q in range(ROWS) for k in (0, 2)])
    return jnp.where(c % 2 == 1, got, x)


def scatter_columns(scattered):
    piece = None
    for j, sent in enumerate(scattered):
        pairs = [(at(4 * k + i, 0), at(4 * i + j, k)) for k in range(COLS) for i in range(4)]
        got = lax.ppermute(sent, PLANE, pairs)
        piece = got if piece is None else piece + got
    return piece


def gather_columns(piece):
    copies = jnp.broadcast_to(piece[None], (ROWS, 72, PIVOTS))
    return lax.all_to_all(copies, "frow", 0, 0, tiled=True)


def sum_over_leaf(parts, leaf):
    near = [(0, 1), (1, 0), (2, 3), (3, 2)]
    far = [(0, 3), (3, 0), (1, 2), (2, 1)]
    upper, lower = first_bits(leaf)
    sends, keeps = parts[0::2], parts[1::2]
    pairs = ((near, far), (far, near))
    first = (upper, lower)
    second = (leaf // 2, leaf % 2)

    def exchange(xs, turn):
        got = []
        for x, p in zip(xs, pairs):
            got.append(lax.ppermute(x, "leaf", p[turn]))
        return got

    def ordered(bit, mine, got):
        return jnp.where(bit == 0, jnp.concatenate([mine, got]), jnp.concatenate([got, mine]))

    got = exchange(sends, 0)
    sums = [x + y for x, y in zip(keeps, got)]
    small = 32
    cut = lambda x, i: lax.dynamic_slice_in_dim(x, i * small, small)
    got = exchange([cut(x, 1 - b) for x, b in zip(sums, second)], 1)
    done = [cut(x, b) + y for x, b, y in zip(sums, second, got)]
    got = exchange(done, 1)
    halved = [ordered(b, x, y) for b, x, y in zip(second, done, got)]
    got = exchange(halved, 0)
    return jnp.concatenate([ordered(b, x, y) for b, x, y in zip(first, halved, got)])


def per_device(child_fronts, parent_front, block_maps):
    leaf = lax.axis_index("leaf")
    r = lax.axis_index("frow")
    c = lax.axis_index("fcol")
    pivots, k, kp, rows, *scattered = pack(child_fronts, parent_front)
    pivots = spread_rows(pivots, r, (8, 4, 2))
    rows = spread_far(rows, c)
    piece = scatter_columns(scattered)
    gathered = gather_columns(piece)
    pivots = spread_rows(pivots, r, (1,))
    pivots = spread_far(pivots, c)
    pivots = spread_core(pivots, c)
    rows = spread_core(rows, c)
    base, high, low, b_rows, k_inv, kp_inv = prepare(
        block_maps, pivots, kp, rows, child_fronts, parent_front
    )
    parts = contribute(block_maps, gathered, k_inv, kp_inv, base, high, low)
    parent_done = sum_over_leaf(parts, leaf)
    finished = finish(b_rows, gathered, k, k_inv, child_fronts)
    return finished, parent_done


def solution(mesh):
    return jax.shard_map(
        per_device,
        mesh=mesh,
        in_specs=(P("leaf", "frow", "fcol"), P("frow", "fcol"), P("leaf", None)),
        out_specs=(P("leaf", "frow", "fcol"), P("frow", "fcol")),
        check_vma=False,
    )
```

```python
import jax
import jax.numpy as jnp
from jax import lax
from jax.experimental import pallas as pl
from jax.experimental.pallas import tpu as pltpu
from jax.sharding import PartitionSpec as P


BLOCK = 128
PIVOTS = 256
STRIP = PIVOTS + BLOCK
PLANE = ("frow", "fcol")
ROWS = 16
COLS = 4
HIGHEST = lax.Precision.HIGHEST
VMEM = pl.BlockSpec(memory_space=pltpu.VMEM)
SMEM = pl.BlockSpec(memory_space=pltpu.SMEM)


def mm(a, b):
    return lax.dot_general(
        a, b, (((1,), (0,)), ((), ())), precision=HIGHEST, preferred_element_type=jnp.float32
    )


def mm_t(a, b):
    return lax.dot_general(
        a, b, (((1,), (1,)), ((), ())), precision=HIGHEST, preferred_element_type=jnp.float32
    )


def halves(x):
    high = x.astype(jnp.bfloat16)
    return high, (x - high.astype(jnp.float32)).astype(jnp.bfloat16)


def product_t(a, b):
    dot = lambda x, y: lax.dot_general(
        x, y, (((1,), (1,)), ((), ())), preferred_element_type=jnp.float32
    )
    (ah, al), (bh, bl) = a, b
    return dot(ah, bh) + (dot(ah, bl) + dot(al, bh))


def f32(*shape):
    return jax.ShapeDtypeStruct(shape, jnp.float32)


def eight_columns(groups, start):
    lane = lax.broadcasted_iota(jnp.int32, (8, BLOCK), 1)
    sub = lax.broadcasted_iota(jnp.int32, (8, BLOCK), 0)
    spread = lambda v: jnp.broadcast_to(v, (8, BLOCK))
    here = start // 8
    inside = (lane >= start) & (lane < start + 8)
    x = groups[here]
    column = [spread(x[:, start + k : start + k + 1]) for k in range(8)]
    s = [[spread(column[k][i : i + 1]) if k <= i else None for k in range(8)] for i in range(8)]
    unit = jnp.where(inside, jnp.where(lane - start == sub, 1.0, 0.0), x)
    line = [spread(unit[k : k + 1]) for k in range(8)]
    inv = [None] * 8
    low = [[None] * 8 for _ in range(8)]
    forward = [None] * 8
    for k in range(8):
        inv[k] = 1.0 / s[k][k]
        for i in range(k + 1, 8):
            low[i][k] = s[i][k] * inv[k]
        for i in range(k + 1, 8):
            for q in range(k + 1, i + 1):
                s[i][q] = s[i][q] - low[i][k] * s[q][k]
        t = line[k]
        for q in range(k):
            t = t - low[k][q] * forward[q]
        forward[k] = t
    back = [None] * 8
    for k in reversed(range(8)):
        t = inv[k] * forward[k]
        for i in range(k + 1, 8):
            t = t - low[i][k] * back[i]
        back[k] = t
    for g in range(here + 1, BLOCK // 8):
        rows = groups[g]
        parts = [spread(rows[:, start + k : start + k + 1]) * back[k] for k in range(8)]
        while len(parts) > 1:
            parts = [parts[i] + parts[i + 1] for i in range(0, len(parts), 2)]
        groups[g] = jnp.where(inside, 0.0, rows) - parts[0]
    own = forward[0] * jnp.sqrt(inv[0])
    for k in range(1, 8):
        own = jnp.where(sub == k, forward[k] * jnp.sqrt(inv[k]), own)
    groups[here] = own


def inverse_factors(blocks):
    split = [[b[8 * g : 8 * g + 8] for g in range(BLOCK // 8)] for b in blocks]
    for start in range(0, BLOCK, 8):
        for groups in split:
            eight_columns(groups, start)
    row, col = square()
    return [jnp.where(col <= row, jnp.concatenate(groups, axis=0), 0.0) for groups in split]


def square():
    shape = (BLOCK, BLOCK)
    return lax.broadcasted_iota(jnp.int32, shape, 0), lax.broadcasted_iota(jnp.int32, shape, 1)


def pack_body(front, parent, pivots, k, kp, rows, *scattered):
    leaf, r, c = lax.axis_index("leaf"), lax.axis_index("frow"), lax.axis_index("fcol")
    rows[:, :PIVOTS] = front[0]
    rows[:, PIVOTS:] = parent[...]
    for j, out in enumerate(scattered):
        out[:64] = front[0, 64 * j : 64 * j + 64]
        at_row = pl.multiple_of(64 * leaf + 16 * j, 8)
        out[64:, :BLOCK] = parent[pl.ds(at_row, 8)]
        out[64:, BLOCK:] = parent[pl.ds(at_row + 8, 8)]
    owner = (r == 0) & (c == 0)

    @pl.when(owner)
    def _():
        row, col = square()
        a11 = front[0, :BLOCK, :BLOCK]
        ap = parent[:BLOCK]
        (k1_inv,) = inverse_factors([a11])
        k21 = mm_t(front[0, BLOCK:, :BLOCK], k1_inv)
        s22 = front[0, BLOCK:, BLOCK:] - mm_t(k21, k21)
        k2_inv, parent_inv = inverse_factors([s22, ap])
        pivots[:BLOCK] = jnp.where(col <= row, k1_inv, k2_inv.T)
        pivots[BLOCK:PIVOTS] = -mm(k2_inv, mm(k21, k1_inv))
        pivots[PIVOTS : PIVOTS + BLOCK] = parent_inv
        strip = mm_t(parent[pl.ds(pl.multiple_of(64 * leaf, 64), 64)], parent_inv)
        pivots[STRIP : STRIP + 64] = jnp.where(leaf < 2, 0.0, strip)
        diag = jnp.sum(jnp.where(row == col, k2_inv, 0.0), axis=0, keepdims=True)
        pivots[STRIP + 64 :] = jnp.broadcast_to(diag, (8, BLOCK))
        k[:BLOCK, :BLOCK] = jnp.where(col <= row, mm_t(a11, k1_inv), 0.0)
        k[:BLOCK, BLOCK:] = jnp.zeros((BLOCK, BLOCK), jnp.float32)
        k[BLOCK:, :BLOCK] = k21
        k[BLOCK:, BLOCK:] = jnp.where(col <= row, mm_t(s22, k2_inv), 0.0)
        kp[...] = jnp.where(col <= row, mm_t(ap, parent_inv), 0.0)

    @pl.when(jnp.logical_not(owner))
    def _():
        for out in (pivots, k, kp):
            out[...] = jnp.zeros_like(out)


def pack(front, parent):
    return pl.pallas_call(
        pack_body,
        grid=(1,),
        in_specs=[
            pl.BlockSpec((1, PIVOTS, PIVOTS), lambda i: (0, 0, 0)),
            pl.BlockSpec((PIVOTS, BLOCK), lambda i: (0, 0)),
        ],
        out_specs=[VMEM] * 8,
        out_shape=[f32(456, BLOCK), f32(PIVOTS, PIVOTS), f32(BLOCK, BLOCK), f32(256, 384)]
        + [f32(72, PIVOTS)] * 4,
        name="pack",
    )(front, parent)


def prepare_body(
    maps, pivots, kp, rows, front, parent, base, high, low, b_rows, k_inv, kp_inv
):
    leaf, r, c = lax.axis_index("leaf"), lax.axis_index("frow"), lax.axis_index("fcol")
    i = pl.program_id(0)
    kept_rows = jnp.where(r > 0, 1.0, 0.0)
    turn = maps[0, 2 * r] % 2

    @pl.when(i == 0)
    def _():
        row, col = square()
        both = pivots[:BLOCK]
        diag = jnp.broadcast_to(pivots[STRIP + 64 : STRIP + 65], (BLOCK, BLOCK))
        k_inv[:BLOCK, :BLOCK] = jnp.where(col <= row, both, 0.0)
        k_inv[:BLOCK, BLOCK:] = jnp.zeros((BLOCK, BLOCK), jnp.float32)
        k_inv[BLOCK:, :BLOCK] = pivots[BLOCK:PIVOTS]
        k_inv[BLOCK:, BLOCK:] = jnp.where(col > row, both, 0.0).T + jnp.where(row == col, diag, 0.0)
        kp_inv[...] = pivots[PIVOTS : PIVOTS + BLOCK]
        b = mm_t(rows[:, :PIVOTS], k_inv[...])
        b_rows[:, :PIVOTS] = b
        b = b * kept_rows
        bp = mm_t(rows[:, PIVOTS:], kp_inv[...])
        b_rows[:, PIVOTS:] = bp
        for h in range(2):
            block = slice(h * BLOCK, (h + 1) * BLOCK)
            to = pl.multiple_of((h + turn) % 2 * BLOCK, BLOCK)
            high[pl.ds(to, BLOCK), :PIVOTS], low[pl.ds(to, BLOCK), :PIVOTS] = halves(b[block])
            mine = bp[block] * kept_rows if h == 0 else bp[block]
            high[block, PIVOTS:], low[block, PIVOTS:] = halves(mine)

    pair = lax.broadcasted_iota(jnp.int32, (1, BLOCK), 1)
    kept = jnp.where((c > 0) | (i > 0), 1.0, 0.0)
    swap = maps[0, 2 * (4 * c + i)] % 2
    for h in range(2):
        from_row = pl.multiple_of((h + turn) % 2 * BLOCK, BLOCK)
        block = slice(h * BLOCK, (h + 1) * BLOCK)
        for g in range(2):
            from_col = pl.multiple_of((g + swap) % 2 * BLOCK, BLOCK)
            strips = slice(g * BLOCK, (g + 1) * BLOCK)
            mine = (2 * g + pair // 64) == leaf
            child = front[0, pl.ds(from_row, BLOCK), pl.ds(from_col, BLOCK)] * (kept_rows * kept)
            theirs = parent[block, strips]
            if h == 0:
                theirs = theirs * kept_rows
            base[block, strips] = child + jnp.where(mine, theirs, 0.0)

    @pl.when((c == 0) & (i == 0))
    def _():
        mine = pair // 64 == leaf
        top = jnp.where(r == 0, kp[...], b_rows[:BLOCK, PIVOTS:])
        base[:BLOCK, :BLOCK] = jnp.where(mine, top, 0.0)
        base[BLOCK:, :BLOCK] = jnp.where(mine, b_rows[BLOCK:, PIVOTS:], 0.0)


def whole(*shape):
    return pl.BlockSpec(shape, lambda i: (0,) * len(shape))


GATHERED = pl.BlockSpec((4, 72, PIVOTS), lambda i: (i, 0, 0))
FRONT = pl.BlockSpec((1, 256, 256), lambda i: (0, 0, i))
PARENT = pl.BlockSpec((256, 256), lambda i: (0, i))


def prepare(maps, pivots, kp, rows, front, parent):
    half = jax.ShapeDtypeStruct((256, 384), jnp.bfloat16)
    return pl.pallas_call(
        prepare_body,
        grid=(4,),
        in_specs=[SMEM, whole(456, BLOCK), whole(BLOCK, BLOCK), whole(256, 384), FRONT, PARENT],
        out_specs=[
            PARENT,
            whole(256, 384),
            whole(256, 384),
            whole(256, 384),
            whole(PIVOTS, PIVOTS),
            whole(BLOCK, BLOCK),
        ],
        out_shape=[f32(256, 1024), half, half, f32(256, 384), f32(PIVOTS, PIVOTS), f32(BLOCK, BLOCK)],
        name="prepare",
    )(maps, pivots, kp, rows, front, parent)


def raw_columns(gathered):
    return jnp.concatenate([gathered[j, :64] for j in range(4)], axis=0)


def contribute_body(maps, gathered, first, k_inv, kp_inv, base, high, low, *rest):
    outs, (columns, value) = rest[:4], rest[4:]
    leaf, c = lax.axis_index("leaf"), lax.axis_index("fcol")
    i = pl.program_id(0)

    @pl.when(i == 0)
    def _():
        columns[:, PIVOTS:] = jnp.zeros((256, BLOCK), jnp.float32)

    kept = jnp.where((c > 0) | (i > 0), 1.0, 0.0)
    swap = maps[0, 2 * (4 * c + i)] % 2
    own = mm_t(raw_columns(gathered), k_inv[...])
    for h in range(2):
        to = pl.multiple_of((h + swap) % 2 * BLOCK, BLOCK)
        columns[pl.ds(to, BLOCK), :PIVOTS] = own[h * BLOCK : (h + 1) * BLOCK] * kept
    strip = jnp.concatenate(
        [gathered[j, 64:, half : half + BLOCK] for j in range(4) for half in (0, BLOCK)], axis=0
    )
    to = pl.multiple_of(64 * leaf, 64)
    columns[pl.ds(to, 64), PIVOTS:] = jnp.where(
        (c == 0) & (i == 0), first[...], mm_t(strip, kp_inv[...])
    )
    value[...] = base[...] - product_t((high[...], low[...]), halves(columns[...]))
    for half, bit in enumerate(first_bits(leaf)):
        for out, at_row in ((outs[2 * half], 1 - bit), (outs[2 * half + 1], bit)):
            out[...] = value[pl.ds(pl.multiple_of(BLOCK * half + 64 * at_row, 64), 64)]


def first_bits(leaf):
    return jnp.where((leaf == 1) | (leaf == 2), 1, 0), leaf // 2


def contribute(maps, gathered, pivots, k_inv, kp_inv, base, high, low):
    return pl.pallas_call(
        contribute_body,
        grid=(4,),
        in_specs=[
            SMEM,
            GATHERED,
            pl.BlockSpec((64, BLOCK), lambda i: (STRIP // 64, 0)),
            whole(PIVOTS, PIVOTS),
            whole(BLOCK, BLOCK),
            PARENT,
            whole(256, 384),
            whole(256, 384),
        ],
        out_specs=[pl.BlockSpec((64, 256), lambda i: (0, i))] * 4,
        out_shape=[f32(64, 1024)] * 4,
        scratch_shapes=[pltpu.VMEM((256, 384), jnp.float32), pltpu.VMEM((256, 256), jnp.float32)],
        name="contribute",
    )(maps, gathered, pivots, k_inv, kp_inv, base, high, low)


def finish_body(b_rows, gathered, k, k_inv, front, out, high, low):
    r, c = lax.axis_index("frow"), lax.axis_index("fcol")
    i = pl.program_id(0)

    @pl.when(i == 0)
    def _():
        high[...], low[...] = halves(b_rows[:, :PIVOTS])

    @pl.when(r == 0)
    def _():
        out[...] = jnp.zeros_like(out)

    @pl.when(r > 0)
    def _():
        own = mm_t(raw_columns(gathered), k_inv[...])
        out[0] = front[0] - product_t((high[...], low[...]), halves(own))

    @pl.when((c == 0) & (i == 0))
    def _():
        out[0] = jnp.where(r == 0, k[...], b_rows[:, :PIVOTS])


def finish(b_rows, gathered, k, k_inv, front):
    return pl.pallas_call(
        finish_body,
        grid=(4,),
        in_specs=[
            whole(256, 384),
            GATHERED,
            whole(PIVOTS, PIVOTS),
            whole(PIVOTS, PIVOTS),
            FRONT,
        ],
        out_specs=FRONT,
        out_shape=f32(1, 256, 1024),
        scratch_shapes=[
            pltpu.VMEM((256, 256), jnp.bfloat16),
            pltpu.VMEM((256, 256), jnp.bfloat16),
        ],
        cost_estimate=pl.CostEstimate(flops=1 << 31, bytes_accessed=4 << 20, transcendentals=0),
        name="finish",
    )(b_rows, gathered, k, k_inv, front)


def at(r, c):
    return r * COLS + c


def spread_rows(x, r, steps):
    for step in steps:
        pairs = [(at(q, 0), at(q + step, 0)) for q in range(0, ROWS, 2 * step)]
        got = lax.ppermute(x, PLANE, pairs)
        x = jnp.where(r % (2 * step) == step, got, x)
    return x


def spread_far(x, c):
    got = lax.ppermute(x, PLANE, [(at(q, 0), at(q, 2)) for q in range(ROWS)])
    return jnp.where(c == 2, got, x)


def spread_core(x, c):
    got = lax.ppermute(x, PLANE, [(at(q, k), at(q, k + 1)) for q in range(ROWS) for k in (0, 2)])
    return jnp.where(c % 2 == 1, got, x)


def scatter_columns(scattered):
    piece = None
    for j, sent in enumerate(scattered):
        pairs = [(at(4 * k + i, 0), at(4 * i + j, k)) for k in range(COLS) for i in range(4) if k + i]
        got = lax.ppermute(sent, PLANE, pairs)
        piece = got if piece is None else piece + got
    return piece


def gather_columns(piece):
    copies = jnp.broadcast_to(piece[None], (ROWS, 72, PIVOTS))
    return lax.all_to_all(copies, "frow", 0, 0, tiled=True)


def sum_over_leaf(parts, leaf):
    near = [(0, 1), (1, 0), (2, 3), (3, 2)]
    far = [(0, 3), (3, 0), (1, 2), (2, 1)]
    sends, keeps = parts[0::2], parts[1::2]
    pairs = ((near, far), (far, near))

    def exchange(xs, turn):
        got = []
        for x, p in zip(xs, pairs):
            got.append(lax.ppermute(x, "leaf", p[turn]))
        return got

    def ordered(bit, mine, got):
        return jnp.where(bit == 0, jnp.concatenate([mine, got]), jnp.concatenate([got, mine]))

    got = exchange(sends, 0)
    sums = [x + y for x, y in zip(keeps, got)]
    got = exchange(sums, 1)
    halved = [x + y for x, y in zip(sums, got)]
    got = exchange(halved, 0)
    return jnp.concatenate([ordered(b, x, y) for b, x, y in zip(first_bits(leaf), halved, got)])


def per_device(child_fronts, parent_front, block_maps):
    leaf = lax.axis_index("leaf")
    r = lax.axis_index("frow")
    c = lax.axis_index("fcol")
    pivots, k, kp, rows, *scattered = pack(child_fronts, parent_front)
    pivots = spread_rows(pivots, r, (8, 4, 2))
    rows = spread_far(rows, c)
    piece = scatter_columns(scattered)
    gathered = gather_columns(piece)
    pivots = spread_rows(pivots, r, (1,))
    pivots = spread_far(pivots, c)
    pivots = spread_core(pivots, c)
    rows = spread_core(rows, c)
    base, high, low, b_rows, k_inv, kp_inv = prepare(
        block_maps, pivots, kp, rows, child_fronts, parent_front
    )
    parts = contribute(block_maps, gathered, pivots, k_inv, kp_inv, base, high, low)
    parent_done = sum_over_leaf(parts, leaf)
    finished = finish(b_rows, gathered, k, k_inv, child_fronts)
    return finished, parent_done


def solution(mesh):
    return jax.shard_map(
        per_device,
        mesh=mesh,
        in_specs=(P("leaf", "frow", "fcol"), P("frow", "fcol"), P("leaf", None)),
        out_specs=(P("leaf", "frow", "fcol"), P("frow", "fcol")),
        check_vma=False,
    )
```

```python
import jax
import jax.numpy as jnp
from jax import lax
from jax.experimental import pallas as pl
from jax.experimental.pallas import tpu as pltpu
from jax.sharding import PartitionSpec as P


BLOCK = 128
PIVOTS = 256
STRIP = PIVOTS + BLOCK
PLANE = ("frow", "fcol")
ROWS = 16
COLS = 4
HIGHEST = lax.Precision.HIGHEST
VMEM = pl.BlockSpec(memory_space=pltpu.VMEM)
SMEM = pl.BlockSpec(memory_space=pltpu.SMEM)


def mm(a, b):
    return lax.dot_general(
        a, b, (((1,), (0,)), ((), ())), precision=HIGHEST, preferred_element_type=jnp.float32
    )


def mm_t(a, b):
    return lax.dot_general(
        a, b, (((1,), (1,)), ((), ())), precision=HIGHEST, preferred_element_type=jnp.float32
    )


def halves(x):
    high = x.astype(jnp.bfloat16)
    return high, (x - high.astype(jnp.float32)).astype(jnp.bfloat16)


def product_t(a, b):
    dot = lambda x, y: lax.dot_general(
        x, y, (((1,), (1,)), ((), ())), preferred_element_type=jnp.float32
    )
    (ah, al), (bh, bl) = a, b
    return dot(ah, bh) + (dot(ah, bl) + dot(al, bh))


def f32(*shape):
    return jax.ShapeDtypeStruct(shape, jnp.float32)


def eight_columns(groups, start):
    lane = lax.broadcasted_iota(jnp.int32, (8, BLOCK), 1)
    sub = lax.broadcasted_iota(jnp.int32, (8, BLOCK), 0)
    spread = lambda v: jnp.broadcast_to(v, (8, BLOCK))
    here = start // 8
    inside = (lane >= start) & (lane < start + 8)
    x = groups[here]
    column = [spread(x[:, start + k : start + k + 1]) for k in range(8)]
    s = [[spread(column[k][i : i + 1]) if k <= i else None for k in range(8)] for i in range(8)]
    unit = jnp.where(inside, jnp.where(lane - start == sub, 1.0, 0.0), x)
    line = [spread(unit[k : k + 1]) for k in range(8)]
    inv = [None] * 8
    low = [[None] * 8 for _ in range(8)]
    forward = [None] * 8
    for k in range(8):
        inv[k] = 1.0 / s[k][k]
        for i in range(k + 1, 8):
            low[i][k] = s[i][k] * inv[k]
        for i in range(k + 1, 8):
            for q in range(k + 1, i + 1):
                s[i][q] = s[i][q] - low[i][k] * s[q][k]
        t = line[k]
        for q in range(k):
            t = t - low[k][q] * forward[q]
        forward[k] = t
    back = [None] * 8
    for k in reversed(range(8)):
        t = inv[k] * forward[k]
        for i in range(k + 1, 8):
            t = t - low[i][k] * back[i]
        back[k] = t
    for g in range(here + 1, BLOCK // 8):
        rows = groups[g]
        parts = [spread(rows[:, start + k : start + k + 1]) * back[k] for k in range(8)]
        while len(parts) > 1:
            parts = [parts[i] + parts[i + 1] for i in range(0, len(parts), 2)]
        groups[g] = jnp.where(inside, 0.0, rows) - parts[0]
    own = forward[0] * jnp.sqrt(inv[0])
    for k in range(1, 8):
        own = jnp.where(sub == k, forward[k] * jnp.sqrt(inv[k]), own)
    groups[here] = own


def inverse_factors(blocks):
    split = [[b[8 * g : 8 * g + 8] for g in range(BLOCK // 8)] for b in blocks]
    for start in range(0, BLOCK, 8):
        for groups in split:
            eight_columns(groups, start)
    row, col = square()
    return [jnp.where(col <= row, jnp.concatenate(groups, axis=0), 0.0) for groups in split]


def square():
    shape = (BLOCK, BLOCK)
    return lax.broadcasted_iota(jnp.int32, shape, 0), lax.broadcasted_iota(jnp.int32, shape, 1)


def pack_body(front, parent, pivots, k, kp, rows, *scattered):
    leaf, r, c = lax.axis_index("leaf"), lax.axis_index("frow"), lax.axis_index("fcol")
    rows[:, :PIVOTS] = front[0]
    rows[:, PIVOTS:] = parent[...]
    for j, out in enumerate(scattered):
        out[:64] = front[0, 64 * j : 64 * j + 64]
        at_row = pl.multiple_of(64 * leaf + 16 * j, 8)
        out[64:, :BLOCK] = parent[pl.ds(at_row, 8)]
        out[64:, BLOCK:] = parent[pl.ds(at_row + 8, 8)]
    owner = (r == 0) & (c == 0)

    @pl.when(owner)
    def _():
        row, col = square()
        a11 = front[0, :BLOCK, :BLOCK]
        ap = parent[:BLOCK]
        (k1_inv,) = inverse_factors([a11])
        k21 = mm_t(front[0, BLOCK:, :BLOCK], k1_inv)
        s22 = front[0, BLOCK:, BLOCK:] - mm_t(k21, k21)
        k2_inv, parent_inv = inverse_factors([s22, ap])
        pivots[:BLOCK] = jnp.where(col <= row, k1_inv, k2_inv.T)
        pivots[BLOCK:PIVOTS] = -mm(k2_inv, mm(k21, k1_inv))
        pivots[PIVOTS : PIVOTS + BLOCK] = parent_inv
        strip = mm_t(parent[pl.ds(pl.multiple_of(64 * leaf, 64), 64)], parent_inv)
        pivots[STRIP : STRIP + 64] = jnp.where(leaf < 2, 0.0, strip)
        diag = jnp.sum(jnp.where(row == col, k2_inv, 0.0), axis=0, keepdims=True)
        pivots[STRIP + 64 :] = jnp.broadcast_to(diag, (8, BLOCK))
        k[:BLOCK, :BLOCK] = jnp.where(col <= row, mm_t(a11, k1_inv), 0.0)
        k[:BLOCK, BLOCK:] = jnp.zeros((BLOCK, BLOCK), jnp.float32)
        k[BLOCK:, :BLOCK] = k21
        k[BLOCK:, BLOCK:] = jnp.where(col <= row, mm_t(s22, k2_inv), 0.0)
        kp[...] = jnp.where(col <= row, mm_t(ap, parent_inv), 0.0)

    @pl.when(jnp.logical_not(owner))
    def _():
        for out in (pivots, k, kp):
            out[...] = jnp.zeros_like(out)


def pack(front, parent):
    return pl.pallas_call(
        pack_body,
        grid=(1,),
        in_specs=[
            pl.BlockSpec((1, PIVOTS, PIVOTS), lambda i: (0, 0, 0)),
            pl.BlockSpec((PIVOTS, BLOCK), lambda i: (0, 0)),
        ],
        out_specs=[VMEM] * 8,
        out_shape=[f32(456, BLOCK), f32(PIVOTS, PIVOTS), f32(BLOCK, BLOCK), f32(256, 384)]
        + [f32(72, PIVOTS)] * 4,
        name="pack",
    )(front, parent)


def prepare_body(
    maps, pivots, kp, rows, front, parent, base, high, low, b_rows, k_inv, kp_inv
):
    leaf, r, c = lax.axis_index("leaf"), lax.axis_index("frow"), lax.axis_index("fcol")
    i = pl.program_id(0)
    kept_rows = jnp.where(r > 0, 1.0, 0.0)
    turn = maps[0, 2 * r] % 2

    @pl.when(i == 0)
    def _():
        row, col = square()
        both = pivots[:BLOCK]
        diag = jnp.broadcast_to(pivots[STRIP + 64 : STRIP + 65], (BLOCK, BLOCK))
        k_inv[:BLOCK, :BLOCK] = jnp.where(col <= row, both, 0.0)
        k_inv[:BLOCK, BLOCK:] = jnp.zeros((BLOCK, BLOCK), jnp.float32)
        k_inv[BLOCK:, :BLOCK] = pivots[BLOCK:PIVOTS]
        k_inv[BLOCK:, BLOCK:] = jnp.where(col > row, both, 0.0).T + jnp.where(row == col, diag, 0.0)
        kp_inv[...] = pivots[PIVOTS : PIVOTS + BLOCK]
        b = mm_t(rows[:, :PIVOTS], k_inv[...])
        b_rows[:, :PIVOTS] = b
        b = b * kept_rows
        bp = mm_t(rows[:, PIVOTS:], kp_inv[...])
        b_rows[:, PIVOTS:] = bp
        for h in range(2):
            block = slice(h * BLOCK, (h + 1) * BLOCK)
            to = pl.multiple_of((h + turn) % 2 * BLOCK, BLOCK)
            high[pl.ds(to, BLOCK), :PIVOTS], low[pl.ds(to, BLOCK), :PIVOTS] = halves(b[block])
            mine = bp[block] * kept_rows if h == 0 else bp[block]
            high[block, PIVOTS:], low[block, PIVOTS:] = halves(mine)

    pair = lax.broadcasted_iota(jnp.int32, (1, BLOCK), 1)
    kept = jnp.where((c > 0) | (i > 0), 1.0, 0.0)
    swap = maps[0, 2 * (4 * c + i)] % 2
    for h in range(2):
        from_row = pl.multiple_of((h + turn) % 2 * BLOCK, BLOCK)
        block = slice(h * BLOCK, (h + 1) * BLOCK)
        for g in range(2):
            from_col = pl.multiple_of((g + swap) % 2 * BLOCK, BLOCK)
            strips = slice(g * BLOCK, (g + 1) * BLOCK)
            mine = (2 * g + pair // 64) == leaf
            child = front[0, pl.ds(from_row, BLOCK), pl.ds(from_col, BLOCK)] * (kept_rows * kept)
            theirs = parent[block, strips]
            if h == 0:
                theirs = theirs * kept_rows
            base[block, strips] = child + jnp.where(mine, theirs, 0.0)

    @pl.when((c == 0) & (i == 0))
    def _():
        mine = pair // 64 == leaf
        top = jnp.where(r == 0, kp[...], b_rows[:BLOCK, PIVOTS:])
        base[:BLOCK, :BLOCK] = jnp.where(mine, top, 0.0)
        base[BLOCK:, :BLOCK] = jnp.where(mine, b_rows[BLOCK:, PIVOTS:], 0.0)


def whole(*shape):
    return pl.BlockSpec(shape, lambda i: (0,) * len(shape))


GATHERED = pl.BlockSpec((4, 72, PIVOTS), lambda i: (i, 0, 0))
FRONT = pl.BlockSpec((1, 256, 256), lambda i: (0, 0, i))
PARENT = pl.BlockSpec((256, 256), lambda i: (0, i))


def prepare(maps, pivots, kp, rows, front, parent):
    half = jax.ShapeDtypeStruct((256, 384), jnp.bfloat16)
    return pl.pallas_call(
        prepare_body,
        grid=(4,),
        in_specs=[SMEM, whole(456, BLOCK), whole(BLOCK, BLOCK), whole(256, 384), FRONT, PARENT],
        out_specs=[
            PARENT,
            whole(256, 384),
            whole(256, 384),
            whole(256, 384),
            whole(PIVOTS, PIVOTS),
            whole(BLOCK, BLOCK),
        ],
        out_shape=[f32(256, 1024), half, half, f32(256, 384), f32(PIVOTS, PIVOTS), f32(BLOCK, BLOCK)],
        name="prepare",
    )(maps, pivots, kp, rows, front, parent)


def raw_columns(gathered):
    return jnp.concatenate([gathered[j, :64] for j in range(4)], axis=0)


def contribute_body(maps, gathered, first, k_inv, kp_inv, base, high, low, *rest):
    outs, (columns, value) = rest[:4], rest[4:]
    leaf, c = lax.axis_index("leaf"), lax.axis_index("fcol")
    i = pl.program_id(0)

    @pl.when(i == 0)
    def _():
        columns[:, PIVOTS:] = jnp.zeros((256, BLOCK), jnp.float32)

    kept = jnp.where((c > 0) | (i > 0), 1.0, 0.0)
    swap = maps[0, 2 * (4 * c + i)] % 2
    own = mm_t(raw_columns(gathered), k_inv[...])
    for h in range(2):
        to = pl.multiple_of((h + swap) % 2 * BLOCK, BLOCK)
        columns[pl.ds(to, BLOCK), :PIVOTS] = own[h * BLOCK : (h + 1) * BLOCK] * kept
    strip = jnp.concatenate(
        [gathered[j, 64:, half : half + BLOCK] for j in range(4) for half in (0, BLOCK)], axis=0
    )
    to = pl.multiple_of(64 * leaf, 64)
    columns[pl.ds(to, 64), PIVOTS:] = jnp.where(
        (c == 0) & (i == 0), first[...], mm_t(strip, kp_inv[...])
    )
    value[...] = base[...] - product_t((high[...], low[...]), halves(columns[...]))
    for half, bit in enumerate(first_bits(leaf)):
        for out, at_row in ((outs[2 * half], 1 - bit), (outs[2 * half + 1], bit)):
            out[...] = value[pl.ds(pl.multiple_of(BLOCK * half + 64 * at_row, 64), 64)]


def first_bits(leaf):
    return jnp.where((leaf == 1) | (leaf == 2), 1, 0), leaf // 2


def contribute(maps, gathered, pivots, k_inv, kp_inv, base, high, low):
    return pl.pallas_call(
        contribute_body,
        grid=(4,),
        in_specs=[
            SMEM,
            GATHERED,
            pl.BlockSpec((64, BLOCK), lambda i: (STRIP // 64, 0)),
            whole(PIVOTS, PIVOTS),
            whole(BLOCK, BLOCK),
            PARENT,
            whole(256, 384),
            whole(256, 384),
        ],
        out_specs=[pl.BlockSpec((64, 256), lambda i: (0, i))] * 4,
        out_shape=[f32(64, 1024)] * 4,
        scratch_shapes=[pltpu.VMEM((256, 384), jnp.float32), pltpu.VMEM((256, 256), jnp.float32)],
        name="contribute",
        compiler_params=pltpu.CompilerParams(vmem_limit_bytes=24 << 20),
    )(maps, gathered, pivots, k_inv, kp_inv, base, high, low)


def finish_body(b_rows, gathered, k, k_inv, front, out, high, low):
    r, c = lax.axis_index("frow"), lax.axis_index("fcol")
    i = pl.program_id(0)

    @pl.when(i == 0)
    def _():
        high[...], low[...] = halves(b_rows[:, :PIVOTS])

    @pl.when(r == 0)
    def _():
        out[...] = jnp.zeros_like(out)

    @pl.when(r > 0)
    def _():
        own = mm_t(raw_columns(gathered), k_inv[...])
        out[0] = front[0] - product_t((high[...], low[...]), halves(own))

    @pl.when((c == 0) & (i == 0))
    def _():
        out[0] = jnp.where(r == 0, k[...], b_rows[:, :PIVOTS])


def finish(b_rows, gathered, k, k_inv, front):
    return pl.pallas_call(
        finish_body,
        grid=(4,),
        in_specs=[
            whole(256, 384),
            GATHERED,
            whole(PIVOTS, PIVOTS),
            whole(PIVOTS, PIVOTS),
            FRONT,
        ],
        out_specs=FRONT,
        out_shape=f32(1, 256, 1024),
        scratch_shapes=[
            pltpu.VMEM((256, 256), jnp.bfloat16),
            pltpu.VMEM((256, 256), jnp.bfloat16),
        ],
        cost_estimate=pl.CostEstimate(flops=1 << 31, bytes_accessed=4 << 20, transcendentals=0),
        name="finish",
        compiler_params=pltpu.CompilerParams(vmem_limit_bytes=24 << 20),
    )(b_rows, gathered, k, k_inv, front)


def at(r, c):
    return r * COLS + c


def spread_rows(x, r, steps):
    for step in steps:
        pairs = [(at(q, 0), at(q + step, 0)) for q in range(0, ROWS, 2 * step)]
        got = lax.ppermute(x, PLANE, pairs)
        x = jnp.where(r % (2 * step) == step, got, x)
    return x


def spread_far(x, c):
    got = lax.ppermute(x, PLANE, [(at(q, 0), at(q, 2)) for q in range(ROWS)])
    return jnp.where(c == 2, got, x)


def spread_core(x, c):
    got = lax.ppermute(x, PLANE, [(at(q, k), at(q, k + 1)) for q in range(ROWS) for k in (0, 2)])
    return jnp.where(c % 2 == 1, got, x)


def scatter_columns(scattered):
    piece = None
    for j, sent in enumerate(scattered):
        pairs = [(at(4 * k + i, 0), at(4 * i + j, k)) for k in range(COLS) for i in range(4) if k + i]
        got = lax.ppermute(sent, PLANE, pairs)
        piece = got if piece is None else piece + got
    return piece


def gather_columns(piece):
    copies = jnp.broadcast_to(piece[None], (ROWS, 72, PIVOTS))
    return lax.all_to_all(copies, "frow", 0, 0, tiled=True)


def sum_over_leaf(parts, leaf):
    near = [(0, 1), (1, 0), (2, 3), (3, 2)]
    far = [(0, 3), (3, 0), (1, 2), (2, 1)]
    sends, keeps = parts[0::2], parts[1::2]
    pairs = ((near, far), (far, near))

    def exchange(xs, turn):
        got = []
        for x, p in zip(xs, pairs):
            got.append(lax.ppermute(x, "leaf", p[turn]))
        return got

    def ordered(bit, mine, got):
        return jnp.where(bit == 0, jnp.concatenate([mine, got]), jnp.concatenate([got, mine]))

    got = exchange(sends, 0)
    sums = [x + y for x, y in zip(keeps, got)]
    got = exchange(sums, 1)
    halved = [x + y for x, y in zip(sums, got)]
    got = exchange(halved, 0)
    return jnp.concatenate([ordered(b, x, y) for b, x, y in zip(first_bits(leaf), halved, got)])


def per_device(child_fronts, parent_front, block_maps):
    leaf = lax.axis_index("leaf")
    r = lax.axis_index("frow")
    c = lax.axis_index("fcol")
    pivots, k, kp, rows, *scattered = pack(child_fronts, parent_front)
    pivots = spread_rows(pivots, r, (8, 4, 2))
    rows = spread_far(rows, c)
    piece = scatter_columns(scattered)
    gathered = gather_columns(piece)
    pivots = spread_rows(pivots, r, (1,))
    pivots = spread_far(pivots, c)
    pivots = spread_core(pivots, c)
    rows = spread_core(rows, c)
    base, high, low, b_rows, k_inv, kp_inv = prepare(
        block_maps, pivots, kp, rows, child_fronts, parent_front
    )
    in_hbm = [pltpu.with_memory_space_constraint(x, pltpu.HBM) for x in (pivots, k_inv, kp_inv, base, high, low)]
    parts = contribute(block_maps, gathered, *in_hbm)
    parent_done = sum_over_leaf(parts, leaf)
    finished = finish(b_rows, gathered, k, k_inv, child_fronts)
    return finished, parent_done


def solution(mesh):
    return jax.shard_map(
        per_device,
        mesh=mesh,
        in_specs=(P("leaf", "frow", "fcol"), P("frow", "fcol"), P("leaf", None)),
        out_specs=(P("leaf", "frow", "fcol"), P("frow", "fcol")),
        check_vma=False,
    )
```
